128 devices in a mesh: ctx: 32 (over y, x, core), head: 4 (over z).
Axes of the slice: x: 4, y: 4, z: 4, core: 2. Of those that a mesh axis runs over, the one named last changes fastest.
Arguments:
- queries: bfloat16 [65536, 4096], P('ctx', 'head'), may hold values from -2 to 2
- key_rows: bfloat16 [65536, 4096], P('ctx', 'head'), may hold values from -2 to 2
- value_rows: bfloat16 [65536, 4096], P('ctx', 'head'), may hold values from -6 to 6
- log_decay: bfloat16 [65536, 32], P('ctx', 'head'), may hold values from -0.4 to 0, as said below
- norm_gain: float32 [4096], P('head'), may hold values from 0.1 to 1.9
- doc_lengths: int32 [64], replicated, may hold values from 1 to 32768, 65536 in all
- packing: int32 [512], replicated, may hold values from 0 to 511, as said below
Outputs:
- mixed: bfloat16 [65536, 4096], P('ctx', 'head')
The draws below stay inside these ranges and needn't reach their ends.
Inputs may be any that keep to these rules, and one draw needn't show every extreme that they name: packing is a permutation of the blocks. Loader block b is block b % 16 of ctx device b // 16; packed block p belongs to owner p // 16. Of the blocks of one loader, each owner receives none or exactly 1. `doc_lengths`: the lengths sum to 65536; the longest is 32768. `log_decay`: negative logarithms of decays.
All inputs are finite; a program needn't handle non-finite values.
Results may differ from the reference program's by a relative error of at most 0.0055.
Values may be sent and summed in bfloat16 or wider, within the bound.
No kernel may reach another device: no remote copies, remote signals or barrier semaphores. Data moves between devices by JAX's collectives and lax.ppermute only.
A program may use at most 192 MiB of HBM per device.

```python
import math
import jax
import jax.numpy as jnp
import numpy as np
from jax import lax

HEADS = 32
HD = 128
BLOCK = 128
SEGMENT_TOKENS = 2048
BLK_DEV = 16
WINDOW_TOKENS = 65536
NBLK = 512
CAP = 1
DOCS = 64
N_CTX = 32


def draw_packing(key, part):
    devices = WINDOW_TOKENS // SEGMENT_TOKENS
    blocks = SEGMENT_TOKENS // BLOCK
    groups = blocks // CAP
    first_key, second_key, third_key = jax.random.split(jax.random.fold_in(key, 11), 3)
    scores = jax.random.permutation(first_key, devices).astype(jnp.int32)
    offset_ids = jnp.arange(devices, dtype=jnp.int32)
    scores = jnp.where(offset_ids == 1, -2, scores)
    scores = jnp.where(offset_ids == devices // 2, -1, scores)
    chosen = jnp.argsort(scores, stable=True)[:groups].astype(jnp.int32)
    document_offsets = jax.random.permutation(third_key, chosen)
    loader = jnp.arange(devices, dtype=jnp.int32)[:, None]
    local = jnp.arange(blocks, dtype=jnp.int32)[None, :]
    owner = (loader + document_offsets[local // CAP]) % devices
    owner_keys = jax.random.split(second_key, devices)
    orders = jax.vmap(lambda single: jax.random.permutation(single, blocks))(owner_keys)
    position = orders[owner, jnp.broadcast_to(local, owner.shape)]
    return (owner * blocks + position).reshape(-1).astype(jnp.int32)


def draw_log_decay(key, part):
    segment_count = jax.random.split(jax.random.fold_in(key, 23), 6)
    share = 0.5
    fast = jax.random.uniform(segment_count[0], (HEADS,)) < share
    fast_rate = jnp.exp(jax.random.uniform(segment_count[1], (HEADS,), minval=math.log(1.0 / 50.0), maxval=math.log(1.0 / 30.0)))
    slow_rate = jnp.exp(jax.random.uniform(segment_count[2], (HEADS,), minval=math.log(0.2 / WINDOW_TOKENS), maxval=math.log(1.2 / WINDOW_TOKENS)))
    base = jnp.where(fast, fast_rate, slow_rate)
    per_block = jnp.exp(jax.random.uniform(segment_count[3], (WINDOW_TOKENS // BLOCK, 1, HEADS), minval=math.log(0.6), maxval=math.log(1.5)))
    per_row = jnp.exp(jax.random.uniform(segment_count[4], (WINDOW_TOKENS // BLOCK, BLOCK, HEADS), minval=math.log(0.7), maxval=math.log(1.4)))
    decay_rate = (base[None, None, :] * per_block * per_row).reshape(WINDOW_TOKENS, HEADS)
    token_span = jax.random.uniform(segment_count[5], (WINDOW_TOKENS, 1)) < 3.0 / WINDOW_TOKENS
    return (-(decay_rate + jnp.where(token_span, 0.29, 0.0))).astype(jnp.bfloat16)


def steps_of(rng, extent, cuts, low, top_value):
    def one(axis_at, shards_of):
        heights = jax.random.uniform(jax.random.fold_in(jax.random.fold_in(rng, 6), axis_at), (shards_of,), jnp.float32, low / len(cuts), top_value / len(cuts))
        return jnp.repeat(jnp.exp(heights), extent[axis_at] // shards_of).reshape((-1,) + (1,) * (len(extent) - axis_at - 1))

    factor_of = one(*cuts[0])
    for cut in cuts[1:]:
        factor_of = factor_of * one(*cut)
    return factor_of


def profile(amount, total, reach, lean):
    portions = [(1 << 20) // math.isqrt(grade ** lean) + 1 for grade in range(2, amount + 1)]
    rest, counts = total - reach - (amount - 1), [1] * (amount - 1)
    while rest > 0:
        movable = [i for i in range(amount - 1) if counts[i] < reach]
        pool, remaining = sum([portions[i] for i in movable]), rest
        for i in movable:
            addition = min(reach - counts[i], max(1, remaining * portions[i] // pool), rest)
            counts[i] = counts[i] + addition
            rest = rest - addition
    return np.array([reach] + counts)


def ragged_sizes(key, count, total, bound, lean):
    if count == 2:
        one = jax.random.randint(key, (), max(1, total - bound), min(bound, total - 1) + 1)
        return jnp.stack([one, total - one])
    sizes = jnp.asarray(profile(count, total, bound, lean), jnp.int32)
    pairs = (count - 1) // 2
    source_of, taker = sizes[1:1 + 2 * pairs:2], sizes[2:2 + 2 * pairs:2]
    room = jnp.minimum(source_of - 1, bound - taker)
    moved = jax.random.randint(jax.random.fold_in(key, 1), (pairs,), 0, 1 << 20) % (room + 1)
    sizes = sizes.at[1:1 + 2 * pairs:2].set(source_of - moved).at[2:2 + 2 * pairs:2].set(taker + moved)
    return sizes[jax.random.permutation(jax.random.fold_in(key, 2), count)]


def normal_values(rng, extent, deviation, most, cuts=(), held_as=jnp.bfloat16):
    values = jax.random.normal(rng, extent, jnp.float32) * deviation
    if len(cuts) > 0:
        values = steps_of(rng, extent, cuts, -0.22, 0.18) * values
    return jnp.clip(values, min=-most, max=most).astype(held_as)


def setup_inputs(seed: int = 0) -> dict:
    seeds = jax.random.split(jax.random.key(seed), 8)
    queries = normal_values(seeds[0], (WINDOW_TOKENS, HEADS * HD), 0.3, 2.0, ((0, 32), (1, 4)))
    key_rows = normal_values(seeds[1], (WINDOW_TOKENS, HEADS * HD), 0.3, 2.0, ((0, 32), (1, 4)))
    value_rows = normal_values(seeds[2], (WINDOW_TOKENS, HEADS * HD), 1.0, 6.0, ((0, 32), (1, 4)))
    log_decay = draw_log_decay(jax.random.fold_in(seeds[7], 71), 0)
    norm_gain = jnp.clip(1.0 + 0.18 * jax.random.normal(seeds[4], (HEADS * HD,), jnp.float32), 0.1, 1.9)
    doc_lengths = ragged_sizes(seeds[5], DOCS, WINDOW_TOKENS, WINDOW_TOKENS // 2, 2).astype(jnp.int32)
    packing = draw_packing(jax.random.fold_in(seeds[7], 71), 0)
    return {"queries": queries, "key_rows": key_rows, "value_rows": value_rows, "log_decay": log_decay, "norm_gain": norm_gain, "doc_lengths": doc_lengths, "packing": packing}


def rounded(values):
    return lax.optimization_barrier(values.astype(jnp.bfloat16)).astype(jnp.float32)

def local_pass(query_blocks, key_blocks, value_blocks, decay_blocks, first, docid):
    length = first.shape[1]
    block_log = jnp.cumsum(decay_blocks.astype(jnp.float32), axis=1)
    block_total = block_log[:, -1, :]
    seen = jnp.cumsum(first, axis=1)
    reach_block = (seen == 0).astype(jnp.float32)
    unbroken = (seen[:, -1] == 0).astype(jnp.float32)
    order = jnp.arange(length)
    causal = order[:, None] >= order[None, :]
    allowed = causal[None] & (docid[:, :, None] == docid[:, None, :])
    by_head = jnp.transpose(block_log, (0, 2, 1))
    gaps = by_head[:, :, :, None] - by_head[:, :, None, :]
    weight = jnp.where(allowed[:, None], jnp.exp(jnp.minimum(gaps, 0.0)), 0.0)
    queries32 = query_blocks.astype(jnp.float32)
    keys_float32 = key_blocks.astype(jnp.float32)
    values32 = value_blocks.astype(jnp.float32)
    scores = jnp.einsum('nthd,nshd->nhts', queries32, keys_float32)
    weights = rounded(scores * weight)
    intra = jnp.einsum('nhts,nshd->nthd', weights, values32)
    same_last = (docid == docid[:, -1:]).astype(jnp.float32)
    keep = jnp.exp(block_total[:, None, :] - block_log) * same_last[:, :, None]
    key_decayed = rounded(keys_float32 * keep[..., None])
    own = jnp.einsum('nshd,nshe->nhde', key_decayed, values32)
    gate = jnp.exp(block_total) * unbroken[:, None]

    def advance(state, item):
        factor, term = item
        return (factor[:, None, None] * state + term, state)
    start = jnp.zeros(own.shape[1:], jnp.float32)
    s_end, states = lax.scan(advance, start, (gate, own))
    query_decayed = rounded(queries32 * (jnp.exp(block_log) * reach_block[:, :, None])[..., None])
    inter = jnp.einsum('nthd,nhde->nthe', query_decayed, rounded(states))
    prior = jnp.cumsum(block_total, axis=0) - block_total
    segment_log = block_log + prior[:, None, :]
    block_starts = seen[:, -1]
    before = jnp.cumsum(block_starts) - block_starts
    reach_segment = (seen + before[:, None] == 0).astype(jnp.float32)
    clean = (jnp.sum(first) == 0).astype(jnp.float32)
    decay_all = jnp.exp(segment_log[-1, -1]) * clean
    return (intra + inter, segment_log, reach_segment, decay_all, s_end)

def reference(queries, key_rows, value_rows, log_decay, norm_gain, doc_lengths, packing):
    width = HEADS * HD
    inverse = jnp.argsort(packing).astype(jnp.int32)

    def pack(values, inner):
        moved = values.reshape(NBLK, BLOCK, values.shape[1])[inverse]
        return moved.reshape((N_CTX, BLK_DEV, BLOCK) + inner)
    query_seg = pack(queries, (HEADS, HD))
    key_seg = pack(key_rows, (HEADS, HD))
    value_seg = pack(value_rows, (HEADS, HD))
    decay_seg = pack(log_decay, (HEADS,))
    starts = jnp.cumsum(doc_lengths) - doc_lengths
    positions = jnp.arange(WINDOW_TOKENS)
    first = jnp.any(positions[:, None] == starts[None, :], axis=1).astype(jnp.int32)
    docid = lax.optimization_barrier(jnp.sum((starts[None, :] <= positions[:, None]).astype(jnp.int32), axis=1)) - 1
    first = first.reshape(N_CTX, BLK_DEV, BLOCK)
    docid = docid.reshape(N_CTX, BLK_DEV, BLOCK)

    def summary(items):
        outcome = local_pass(*items)
        return (outcome[3], outcome[4])
    decays, ends = lax.map(summary, (query_seg, key_seg, value_seg, decay_seg, first, docid))

    def handoff(state, item):
        factor, term = item
        return (factor[:, None, None] * state + term, state)
    zero_state = jnp.zeros((HEADS, HD, HD), jnp.float32)
    last_state, incoming = lax.scan(handoff, zero_state, (decays, ends))

    def finish(items):
        query_blocks = items[0]
        arrival = items[6]
        local_out, segment_log, reach_segment, decay_all, s_end = local_pass(*items[:6])
        scaled = rounded(query_blocks.astype(jnp.float32) * (jnp.exp(segment_log) * reach_segment[:, :, None])[..., None])
        carried = jnp.einsum('nthd,hde->nthe', scaled, rounded(arrival))
        total = (local_out + carried).reshape(SEGMENT_TOKENS, width)
        square_mean = lax.optimization_barrier(jnp.mean(total * total, axis=1, keepdims=True))
        return (total / jnp.sqrt(square_mean + 1e-05) * norm_gain[None, :]).astype(jnp.bfloat16)
    result = lax.map(finish, (query_seg, key_seg, value_seg, decay_seg, first, docid, incoming))
    return result.reshape(WINDOW_TOKENS, width)
```

```python
import jax
import jax.numpy as jnp
from jax import lax
from jax.experimental import pallas as pl
from jax.experimental.pallas import tpu as pltpu
from jax.sharding import PartitionSpec as P

BLOCK = 128
CHUNKS = 2
FAR = 1e9
F32 = jnp.float32
BF16 = jnp.bfloat16


def dot(a, b, contract):
    return lax.dot_general(a, b, ((contract[:1], contract[1:]), ((), ())), preferred_element_type=F32)


def triangle(upper):
    row = lax.broadcasted_iota(jnp.int32, (BLOCK, BLOCK), 0)
    column = lax.broadcasted_iota(jnp.int32, (BLOCK, BLOCK), 1)
    keep = row <= column if upper else column <= row
    return jnp.where(keep, 1.0, 0.0).astype(BF16)


def log_rows(decay):
    return dot(decay, triangle(True), (0, 0))


def log_columns(decay):
    return dot(triangle(False), decay, (1, 0))


def last_starts(starts, base):
    at = lax.broadcasted_iota(jnp.int32, (BLOCK, BLOCK), 0).astype(F32) + base
    begun = jnp.broadcast_to(starts, (BLOCK, BLOCK))
    return jnp.max(jnp.where(begun <= at, begun, -FAR), axis=1, keepdims=True)


def own_kernel(heads, chunk, packing, place, starts, keys, values, decay, *outs):
    block = pl.program_id(0)
    base = (packing[place[0] * pl.num_programs(0) + block] * BLOCK).astype(F32)
    logs = log_rows(decay[...])
    total = logs[:, BLOCK - 1 :]
    started = last_starts(starts[...], base)[BLOCK - 1 :, :]
    at = lax.broadcasted_iota(jnp.int32, (1, BLOCK), 1).astype(F32) + base
    keep = jnp.exp(total - logs) * jnp.where(at >= started, 1.0, 0.0)
    pieces = outs[0].shape[2]
    per_head = BLOCK // pieces
    for head in range(heads):
        span = slice(head * BLOCK, (head + 1) * BLOCK)
        wide = chunk * heads + head
        faded = keys[:, span].T.astype(F32) * keep[wide : wide + 1, :]
        own = dot(faded.astype(BF16), values[:, span], (1, 0)).astype(BF16)
        outs[0][head * per_head : (head + 1) * per_head, 0] = own.reshape(per_head, pieces, BLOCK)
    if len(outs) > 1:
        gate = jnp.exp(total) * jnp.where(started < base, 1.0, 0.0)
        lane = lax.broadcasted_iota(jnp.int32, outs[1].shape, 1)

        @pl.when(block == 0)
        def _():
            outs[1][...] = jnp.zeros(outs[1].shape, F32)

        outs[1][...] = jnp.where(lane == block, gate, outs[1][...])


def own_states(chunk, packing, place, starts, keys, values, decay):
    rows, width = keys.shape
    all_heads = decay.shape[1]
    blocks = rows // BLOCK
    heads = all_heads // CHUNKS
    columns = width // CHUNKS
    devices = packing.shape[0] // blocks
    pieces = heads * BLOCK // devices
    outs = [jax.ShapeDtypeStruct((devices, blocks, pieces, BLOCK), BF16)]
    specs = [pl.BlockSpec((devices, 1, pieces, BLOCK), lambda b, *_: (0, b, 0, 0))]
    if chunk == 0:
        outs.append(jax.ShapeDtypeStruct((all_heads, BLOCK), F32))
        specs.append(pl.BlockSpec((all_heads, BLOCK), lambda b, *_: (0, 0)))
    return pl.pallas_call(
        lambda *refs: own_kernel(heads, chunk, *refs),
        grid_spec=pltpu.PrefetchScalarGridSpec(
            num_scalar_prefetch=2,
            grid=(blocks,),
            in_specs=[
                pl.BlockSpec((1, BLOCK), lambda b, *_: (0, 0)),
                pl.BlockSpec((BLOCK, columns), lambda b, *_: (b, chunk)),
                pl.BlockSpec((BLOCK, columns), lambda b, *_: (b, chunk)),
                pl.BlockSpec((BLOCK, all_heads), lambda b, *_: (b, 0)),
            ],
            out_specs=specs,
        ),
        out_shape=outs,
        name=f"own{chunk}",
    )(packing, place, starts, keys, values, decay)


def intra_kernel(heads, packing, place, starts, queries, keys, values, decay, intra, faded):
    block = pl.program_id(0)
    base = (packing[place[0] * pl.num_programs(0) + block] * BLOCK).astype(F32)
    along = log_rows(decay[...])
    down = log_columns(decay[...])
    started = last_starts(starts[...], base)
    row = lax.broadcasted_iota(jnp.int32, (BLOCK, BLOCK), 0)
    column = lax.broadcasted_iota(jnp.int32, (BLOCK, BLOCK), 1)
    allowed = (column <= row) & (column.astype(F32) + base >= started)
    reach = jnp.exp(down) * jnp.where(started < base, 1.0, 0.0)
    for head in range(heads):
        span = slice(head * BLOCK, (head + 1) * BLOCK)
        query = queries[:, span]
        scores = dot(query, keys[:, span], (1, 1))
        gaps = jnp.minimum(down[:, head : head + 1] - along[head : head + 1, :], 0.0)
        weights = (scores * jnp.where(allowed, jnp.exp(gaps), 0.0)).astype(BF16)
        intra[:, span] = dot(weights, values[:, span], (1, 0))
        faded[:, span] = (query.astype(F32) * reach[:, head : head + 1]).astype(BF16)


def intra_pass(packing, place, starts, queries, keys, values, decay):
    rows, width = queries.shape
    heads = decay.shape[1]
    row_block = pl.BlockSpec((BLOCK, width), lambda b, *_: (b, 0))
    return pl.pallas_call(
        lambda *refs: intra_kernel(heads, *refs),
        grid_spec=pltpu.PrefetchScalarGridSpec(
            num_scalar_prefetch=2,
            grid=(rows // BLOCK,),
            in_specs=[
                pl.BlockSpec((1, BLOCK), lambda b, *_: (0, 0)),
                row_block,
                row_block,
                row_block,
                pl.BlockSpec((BLOCK, heads), lambda b, *_: (b, 0)),
            ],
            out_specs=[row_block, row_block],
        ),
        out_shape=[
            jax.ShapeDtypeStruct((rows, width), F32),
            jax.ShapeDtypeStruct((rows, width), BF16),
        ],
        name="intra",
    )(packing, place, starts, queries, keys, values, decay)


def scan_kernel(order, gates, own, prior):
    def step(j, state):
        at = order[j]
        prior[at] = state.astype(BF16)
        return gates[at] * state + own[at].astype(F32)

    lax.fori_loop(0, own.shape[0], step, jnp.zeros(own.shape[1:], F32), unroll=8)


def scan_pass(order, gates, own, name):
    devices, blocks, pieces, lanes = own.shape
    flat = own.reshape(devices * blocks, pieces, lanes)
    smem = pl.BlockSpec(memory_space=pltpu.SMEM)
    vmem = pl.BlockSpec(memory_space=pltpu.VMEM)
    prior = pl.pallas_call(
        scan_kernel,
        in_specs=[smem, smem, vmem],
        out_specs=vmem,
        out_shape=jax.ShapeDtypeStruct(flat.shape, BF16),
        name=name,
    )(order, gates, flat)
    return prior.reshape(own.shape)


def outgo_kernel(heads, packing, place, faded, intra, states, *refs):
    slots, squares = refs[-2:]
    sums = jnp.zeros((BLOCK, BLOCK), F32)
    per_head = states.shape[0] // heads
    for head in range(heads):
        span = slice(head * BLOCK, (head + 1) * BLOCK)
        state = states[head * per_head : (head + 1) * per_head, 0].reshape(BLOCK, BLOCK)
        out = intra[:, span] + dot(faded[:, span], state, (1, 0))
        sums = sums + out * out
        slots[0, :, span] = out.astype(BF16)
    mine = jnp.broadcast_to(jnp.sum(sums.T, axis=0, keepdims=True), squares.shape[1:])
    squares[0] = mine if len(refs) == 2 else mine + refs[0][0]


def outgo_pass(chunk, packing, place, faded, intra, states, earlier):
    rows, width = faded.shape
    blocks = rows // BLOCK
    devices, _, pieces, lanes = states.shape
    columns = width // CHUNKS
    heads = columns // BLOCK

    def owner(b, packing, place):
        return packing[place[0] * blocks + b] // blocks, 0, 0

    square_block = pl.BlockSpec((1, 8, BLOCK), owner)
    ins = [packing, place, faded, intra, states] + ([] if earlier is None else [earlier])
    return pl.pallas_call(
        lambda *refs: outgo_kernel(heads, *refs),
        grid_spec=pltpu.PrefetchScalarGridSpec(
            num_scalar_prefetch=2,
            grid=(blocks,),
            in_specs=[
                pl.BlockSpec((BLOCK, columns), lambda b, *_: (b, chunk)),
                pl.BlockSpec((BLOCK, columns), lambda b, *_: (b, chunk)),
                pl.BlockSpec((devices, 1, pieces, lanes), lambda b, *_: (0, b, 0, 0)),
            ]
            + ([] if earlier is None else [square_block]),
            out_specs=[pl.BlockSpec((1, BLOCK, columns), owner), square_block],
        ),
        out_shape=[
            jax.ShapeDtypeStruct((devices, BLOCK, columns), BF16),
            jax.ShapeDtypeStruct((devices, 8, BLOCK), F32),
        ],
        name=f"outgo{chunk}",
    )(*ins)


def finish_kernel(width_all, order, place, squares, gain, *refs):
    mixed = refs[-1]
    total = squares[0, 0, :1, :]
    for group in range(1, squares.shape[0]):
        total = total + squares[group, 0, :1, :]
    scale = lax.rsqrt(total / width_all + 1e-05)
    scale = jnp.broadcast_to(scale, (BLOCK, BLOCK)).T
    at = 0
    for part in refs[:-1]:
        for inside in range(part.shape[2] // BLOCK):
            span = slice(inside * BLOCK, (inside + 1) * BLOCK)
            wide = slice(at, at + BLOCK)
            out = part[0, :, span].astype(F32) * scale * gain[:, wide]
            mixed[:, wide] = out.astype(BF16)
            at += BLOCK


def finish_pass(order, place, squares, gain, parts, width_all):
    devices, _, columns = parts[0].shape
    blocks = order.shape[0] // devices
    width = gain.shape[1]

    def loader(b, order, place):
        return order[place[0] * blocks + b] // blocks

    return pl.pallas_call(
        lambda *refs: finish_kernel(width_all, *refs),
        grid_spec=pltpu.PrefetchScalarGridSpec(
            num_scalar_prefetch=2,
            grid=(blocks,),
            in_specs=[
                pl.BlockSpec(
                    (squares.shape[0], 1, 8, BLOCK), lambda b, *s: (0, loader(b, *s), 0, 0)
                ),
                pl.BlockSpec((1, width), lambda b, *_: (0, 0)),
            ]
            + [pl.BlockSpec((1, BLOCK, columns), lambda b, *s: (loader(b, *s), 0, 0))] * len(parts),
            out_specs=pl.BlockSpec((BLOCK, width), lambda b, *_: (b, 0)),
        ),
        out_shape=jax.ShapeDtypeStruct((blocks * BLOCK, width), BF16),
        name="finish",
    )(order, place, squares, gain, *parts)


def swap(x, axis):
    return lax.all_to_all(x, axis, split_axis=0, concat_axis=0, tiled=True)


def body(queries, key_rows, value_rows, log_decay, norm_gain, doc_lengths, packing):
    rows, width = queries.shape
    heads = log_decay.shape[1]
    blocks = rows // BLOCK
    devices = lax.axis_size("ctx")
    mine = lax.axis_index("ctx").astype(jnp.int32)
    place = mine.reshape(1)
    starts = (jnp.cumsum(doc_lengths) - doc_lengths).astype(F32)
    starts = jnp.pad(starts, (0, BLOCK - starts.shape[0]), constant_values=FAR)[None, :]

    own, gates = [], None
    for chunk in range(CHUNKS):
        made = own_states(chunk, packing, place, starts, key_rows, value_rows, log_decay)
        if chunk == 0:
            gates = swap(jnp.broadcast_to(made[1][None], (devices, heads, BLOCK)), "ctx")
        own.append(swap(made[0], "ctx"))
    intra, faded = intra_pass(packing, place, starts, queries, key_rows, value_rows, log_decay)

    total_blocks = packing.shape[0]
    index = jnp.arange(total_blocks, dtype=jnp.int32)
    hit = (packing[None, :] == index[:, None]).astype(jnp.int32)
    order = jnp.sum(hit * index[None, :], axis=1)

    per_head = devices * CHUNKS // heads
    states = []
    for chunk in range(CHUNKS):
        head = chunk * (heads // CHUNKS) + mine // per_head
        gate = lax.dynamic_index_in_dim(gates, head, 1, keepdims=False)[:, :blocks].reshape(-1)
        states.append(swap(scan_pass(order, gate, own[chunk], f"scan{chunk}"), "ctx"))

    parts, squares = [], None
    for chunk in range(CHUNKS):
        slots, squares = outgo_pass(chunk, packing, place, faded, intra, states[chunk], squares)
        parts.append(swap(slots, "ctx"))
    squares = swap(squares, "ctx")
    groups = lax.axis_size("head")
    squares = swap(jnp.broadcast_to(squares[None], (groups,) + squares.shape), "head")
    return finish_pass(order, place, squares, norm_gain[None, :], parts, width * groups)


def solution(mesh):
    placed = (
        P("ctx", "head"),
        P("ctx", "head"),
        P("ctx", "head"),
        P("ctx", "head"),
        P("head"),
        P(),
        P(),
    )
    return jax.shard_map(
        body, mesh=mesh, in_specs=placed, out_specs=P("ctx", "head"), check_vma=False
    )
```

```python
import jax
import jax.numpy as jnp
from jax import lax
from jax.experimental import pallas as pl
from jax.experimental.pallas import tpu as pltpu
from jax.sharding import PartitionSpec as P

BLOCK = 128
EXTRA = 16
FAR = 1e9
F32 = jnp.float32
BF16 = jnp.bfloat16


def dot(a, b, contract):
    return lax.dot_general(a, b, ((contract[:1], contract[1:]), ((), ())), preferred_element_type=F32)


def triangle(upper):
    row = lax.broadcasted_iota(jnp.int32, (BLOCK, BLOCK), 0)
    column = lax.broadcasted_iota(jnp.int32, (BLOCK, BLOCK), 1)
    keep = row <= column if upper else column <= row
    return jnp.where(keep, 1.0, 0.0).astype(BF16)


def in_three(x):
    high = x.astype(BF16).astype(F32)
    middle = (x - high).astype(BF16).astype(F32)
    return high, middle, x - high - middle


def own_kernel(heads, blocks, each, packing, place, starts, keys, values, decay, own, made, fates, sems):
    step = pl.program_id(0)
    per_head = made.shape[0] // heads
    pieces = BLOCK // per_head
    steps = blocks // each
    upper = triangle(True)
    lane = lax.broadcasted_iota(jnp.int32, (1, BLOCK), 1).astype(F32)
    for inside in range(each):
        block = step * each + inside
        rows = slice(inside * BLOCK, (inside + 1) * BLOCK)
        base = (packing[place[0] * blocks + block] * BLOCK).astype(F32)
        logs = dot(decay[:, rows], upper, (1, 0))
        total = logs[:, BLOCK - 1 :]
        begun = jnp.where(starts[...] <= base + (BLOCK - 1), starts[...], -FAR)
        started = jnp.max(begun, axis=1, keepdims=True)
        keep = jnp.exp(total - logs) * jnp.where(lane + base >= started, 1.0, 0.0)
        gate = jnp.exp(total) * jnp.where(started < base, 1.0, 0.0)
        to = pl.ds(pl.multiple_of(block * pieces, pieces), pieces)
        for head in range(heads):
            span = slice(head * BLOCK, (head + 1) * BLOCK)
            faded = keys[rows, span].T.astype(F32) * keep[head : head + 1, :]
            state = dot(faded.astype(BF16), values[rows, span], (1, 0)).astype(BF16)
            made[head * per_head : (head + 1) * per_head, to] = state.reshape(per_head, pieces, BLOCK)
            fates[head, pl.ds(block, 1), :] = jnp.broadcast_to(gate[head : head + 1, :], (1, BLOCK))

    def copy(at, start, size):
        part = (slice(None), pl.ds(start, size))
        return pltpu.make_async_copy(made.at[part], own.at[part], sems.at[at])

    span = each * pieces
    copy(step, pl.multiple_of(step * span, span), span).start()

    @pl.when(step == steps - 1)
    def _():
        at = lax.broadcasted_iota(jnp.int32, (EXTRA, BLOCK), 1)
        for head in range(heads):
            high, middle, low = in_three(fates[head])
            tile = jnp.where(at == 0, high, jnp.where(at == 1, middle, low)).astype(BF16)
            for piece in range(per_head):
                made[head * per_head + piece, blocks * pieces :] = tile
        copy(steps, blocks * pieces, EXTRA).start()
        for earlier in range(steps):
            copy(earlier, earlier * span, span).wait()
        copy(steps, blocks * pieces, EXTRA).wait()


def own_states(packing, place, starts, keys, values, decay):
    rows, width = keys.shape
    heads = decay.shape[0]
    blocks = rows // BLOCK
    each = 4
    devices = packing.shape[0] // blocks
    pieces = heads * BLOCK // devices
    shape = (devices, blocks * pieces + EXTRA, BLOCK)
    row_block = pl.BlockSpec((each * BLOCK, width), lambda b, *_: (b, 0))
    return pl.pallas_call(
        lambda *refs: own_kernel(heads, blocks, each, *refs),
        grid_spec=pltpu.PrefetchScalarGridSpec(
            num_scalar_prefetch=2,
            grid=(blocks // each,),
            in_specs=[
                pl.BlockSpec((1, BLOCK), lambda b, *_: (0, 0)),
                row_block,
                row_block,
                pl.BlockSpec((heads, each * BLOCK), lambda b, *_: (0, b)),
            ],
            out_specs=pl.BlockSpec(memory_space=pl.ANY),
            scratch_shapes=[
                pltpu.VMEM(shape, BF16),
                pltpu.VMEM((heads, blocks, BLOCK), F32),
                pltpu.SemaphoreType.DMA((blocks // each + 1,)),
            ],
        ),
        out_shape=jax.ShapeDtypeStruct(shape, BF16),
        name="own",
    )(packing, place, starts, keys, values, decay)


def intra_kernel(heads, packing, place, starts, queries, keys, values, decay, intra, faded):
    block = pl.program_id(0)
    base = (packing[place[0] * pl.num_programs(0) + block] * BLOCK).astype(F32)
    along = dot(decay[...], triangle(True), (1, 0))
    down = dot(triangle(False), decay[...], (1, 1))
    row = lax.broadcasted_iota(jnp.int32, (BLOCK, BLOCK), 0)
    column = lax.broadcasted_iota(jnp.int32, (BLOCK, BLOCK), 1)
    begun = jnp.broadcast_to(starts[...], (BLOCK, BLOCK))
    begun = jnp.where(begun <= row.astype(F32) + base, begun, -FAR)
    started = jnp.max(begun, axis=1, keepdims=True)
    allowed = (column <= row) & (column.astype(F32) + base >= started)
    reach = jnp.exp(down) * jnp.where(started < base, 1.0, 0.0)
    for head in range(heads):
        span = slice(head * BLOCK, (head + 1) * BLOCK)
        query = queries[:, span]
        scores = dot(query, keys[:, span], (1, 1))
        gaps = jnp.minimum(down[:, head : head + 1] - along[head : head + 1, :], 0.0)
        weights = (scores * jnp.where(allowed, jnp.exp(gaps), 0.0)).astype(BF16)
        intra[:, span] = dot(weights, values[:, span], (1, 0))
        faded[:, span] = (query.astype(F32) * reach[:, head : head + 1]).astype(BF16)


def intra_pass(packing, place, starts, queries, keys, values, decay):
    rows, width = queries.shape
    heads = decay.shape[0]
    row_block = pl.BlockSpec((BLOCK, width), lambda b, *_: (b, 0))
    return pl.pallas_call(
        lambda *refs: intra_kernel(heads, *refs),
        grid_spec=pltpu.PrefetchScalarGridSpec(
            num_scalar_prefetch=2,
            grid=(rows // BLOCK,),
            in_specs=[
                pl.BlockSpec((1, BLOCK), lambda b, *_: (0, 0)),
                row_block,
                row_block,
                row_block,
                pl.BlockSpec((heads, BLOCK), lambda b, *_: (0, b)),
            ],
            out_specs=[row_block, row_block],
        ),
        out_shape=[
            jax.ShapeDtypeStruct((rows, width), F32),
            jax.ShapeDtypeStruct((rows, width), BF16),
        ],
        name="intra",
    )(packing, place, starts, queries, keys, values, decay)


def scan_kernel(blocks, order, own, prior, gates):
    devices, height, _ = prior.shape
    pieces = height // blocks
    for device in range(devices):
        tile = own[device, height:, :].astype(F32)
        gate = tile[:, 0:1] + tile[:, 1:2] + tile[:, 2:3]
        gates[device] = jnp.broadcast_to(gate[:blocks], (blocks, BLOCK))

    def step(j, state):
        at = order[j]
        device, block = at // blocks, at % blocks
        rows = pl.ds(pl.multiple_of(block * pieces, pieces), pieces)
        prior[device, rows, :] = state.astype(BF16)
        return gates[device, pl.ds(block, 1), :] * state + own[device, rows, :].astype(F32)

    lax.fori_loop(0, devices * blocks, step, jnp.zeros((pieces, BLOCK), F32), unroll=8)


def scan_pass(order, own):
    devices, height, lanes = own.shape
    blocks = order.shape[0] // devices
    vmem = pl.BlockSpec(memory_space=pltpu.VMEM)
    return pl.pallas_call(
        lambda *refs: scan_kernel(blocks, *refs),
        in_specs=[pl.BlockSpec(memory_space=pltpu.SMEM), vmem],
        out_specs=vmem,
        out_shape=jax.ShapeDtypeStruct((devices, height - EXTRA, lanes), BF16),
        scratch_shapes=[pltpu.VMEM((devices, blocks, BLOCK), F32)],
        name="scan",
    )(order, own)


def outgo_kernel(heads, blocks, each, packing, place, faded, intra, states, slots, made, sems):
    step = pl.program_id(0)
    per_head = states.shape[0] // heads
    pieces = BLOCK // per_head
    row = lax.broadcasted_iota(jnp.int32, (EXTRA, BLOCK), 0)

    def copy(block):
        owner = packing[place[0] * blocks + block] // blocks
        return pltpu.make_async_copy(made.at[block], slots.at[owner], sems.at[block])

    for inside in range(each):
        block = step * each + inside
        rows = slice(inside * BLOCK, (inside + 1) * BLOCK)
        sums = jnp.zeros((BLOCK, BLOCK), F32)
        for head in range(heads):
            span = slice(head * BLOCK, (head + 1) * BLOCK)
            state = states[
                head * per_head : (head + 1) * per_head, inside * pieces : (inside + 1) * pieces
            ].reshape(BLOCK, BLOCK)
            out = intra[rows, span] + dot(faded[rows, span], state, (1, 0))
            sums = sums + out * out
            made[block, span, :] = out.astype(BF16)
        high, middle, low = in_three(jnp.sum(sums.T, axis=0, keepdims=True))
        tile = jnp.where(row == 0, high, jnp.where(row == 1, middle, low))
        made[block, heads * BLOCK :, :] = tile.astype(BF16)
        copy(block).start()

    @pl.when(step == pl.num_programs(0) - 1)
    def _():
        for block in range(blocks):
            copy(block).wait()


def outgo_pass(packing, place, faded, intra, states):
    rows, width = faded.shape
    blocks = rows // BLOCK
    devices, height, lanes = states.shape
    each = 2
    heads = width // BLOCK
    row_block = pl.BlockSpec((each * BLOCK, width), lambda b, *_: (b, 0))
    return pl.pallas_call(
        lambda *refs: outgo_kernel(heads, blocks, each, *refs),
        grid_spec=pltpu.PrefetchScalarGridSpec(
            num_scalar_prefetch=2,
            grid=(blocks // each,),
            in_specs=[
                row_block,
                row_block,
                pl.BlockSpec((devices, height // blocks * each, lanes), lambda b, *_: (0, b, 0)),
            ],
            out_specs=pl.BlockSpec(memory_space=pl.ANY),
            scratch_shapes=[
                pltpu.VMEM((blocks, width + EXTRA, BLOCK), BF16),
                pltpu.SemaphoreType.DMA((blocks,)),
            ],
        ),
        out_shape=jax.ShapeDtypeStruct((devices, width + EXTRA, BLOCK), BF16),
        name="outgo",
    )(packing, place, faded, intra, states)


def squares_kernel(order, place, came, squares, tiles, sems):
    blocks, extra, _ = tiles.shape
    height = came.shape[1] - extra

    def copy(block):
        loader = order[place[0] * blocks + block] // blocks
        return pltpu.make_async_copy(came.at[loader, height:], tiles.at[block], sems.at[block])

    for block in range(blocks):
        copy(block).start()
    for block in range(blocks):
        copy(block).wait()
        tile = tiles[block].astype(F32)
        squares[block : block + 1, :] = tile[0:1, :] + tile[1:2, :] + tile[2:3, :]


def squares_pass(order, place, came):
    blocks = order.shape[0] // came.shape[0]
    smem = pl.BlockSpec(memory_space=pltpu.SMEM)
    return pl.pallas_call(
        squares_kernel,
        in_specs=[smem, smem, pl.BlockSpec(memory_space=pl.ANY)],
        out_specs=pl.BlockSpec(memory_space=pltpu.VMEM),
        out_shape=jax.ShapeDtypeStruct((blocks, BLOCK), F32),
        scratch_shapes=[
            pltpu.VMEM((blocks, EXTRA, BLOCK), BF16),
            pltpu.SemaphoreType.DMA((blocks,)),
        ],
        name="squares",
    )(order, place, came)


def finish_kernel(groups, each, order, place, *refs):
    squares, gain, parts, mixed = refs[:groups], refs[groups], refs[groups + 1 : -1], refs[-1]
    width = gain.shape[1]
    for inside in range(each):
        block = pl.ds(pl.program_id(0) * each + inside, 1)
        total = squares[0][block, :]
        for other in squares[1:]:
            total = total + other[block, :]
        scale = lax.rsqrt(total / (width * groups) + 1e-05)
        scale = jnp.broadcast_to(scale, (BLOCK, BLOCK)).T
        rows = slice(inside * BLOCK, (inside + 1) * BLOCK)
        for head in range(width // BLOCK):
            span = slice(head * BLOCK, (head + 1) * BLOCK)
            out = parts[inside][0, span, :].astype(F32) * scale * gain[:, span]
            mixed[rows, span] = out.astype(BF16)


def finish_pass(order, place, squares, gain, came):
    devices, height, lanes = came.shape
    blocks = order.shape[0] // devices
    width = gain.shape[1]
    each = 4

    def part(inside):
        def loader(b, order, place):
            return order[place[0] * blocks + b * each + inside] // blocks, 0, 0

        return pl.BlockSpec((1, width, lanes), loader)

    return pl.pallas_call(
        lambda *refs: finish_kernel(len(squares), each, *refs),
        grid_spec=pltpu.PrefetchScalarGridSpec(
            num_scalar_prefetch=2,
            grid=(blocks // each,),
            in_specs=[pl.BlockSpec((blocks, BLOCK), lambda b, *_: (0, 0))] * len(squares)
            + [pl.BlockSpec((1, width), lambda b, *_: (0, 0))]
            + [part(inside) for inside in range(each)],
            out_specs=pl.BlockSpec((each * BLOCK, width), lambda b, *_: (b, 0)),
        ),
        out_shape=jax.ShapeDtypeStruct((blocks * BLOCK, width), BF16),
        name="finish",
    )(order, place, *squares, gain, *[came] * each)


def swap(x, axis):
    return lax.all_to_all(x, axis, split_axis=0, concat_axis=0, tiled=True)


def body(queries, key_rows, value_rows, log_decay, norm_gain, doc_lengths, packing):
    mine = lax.axis_index("ctx").astype(jnp.int32)
    place = mine.reshape(1)
    decay = log_decay.T
    document = jnp.arange(doc_lengths.shape[0], dtype=jnp.int32)
    ahead = document[:, None] < jnp.arange(BLOCK, dtype=jnp.int32)[None, :]
    starts = jnp.sum(jnp.where(ahead, doc_lengths[:, None], 0), axis=0, keepdims=True).astype(F32)

    own = swap(own_states(packing, place, starts, key_rows, value_rows, decay), "ctx")
    intra, faded = intra_pass(packing, place, starts, queries, key_rows, value_rows, decay)

    index = jnp.arange(packing.shape[0], dtype=jnp.int32)
    hit = (packing[None, :] == index[:, None]).astype(jnp.int32)
    order = jnp.sum(hit * index[None, :], axis=1)

    states = swap(scan_pass(order, own), "ctx")
    came = swap(outgo_pass(packing, place, faded, intra, states), "ctx")
    part = squares_pass(order, place, came)
    groups = lax.axis_size("head")
    squares = [part]
    for shift in range(1, groups):
        pairs = [(i, (i + shift) % groups) for i in range(groups)]
        squares.append(lax.ppermute(part, "head", pairs))
    return finish_pass(order, place, squares, norm_gain[None, :], came)


def solution(mesh):
    placed = (
        P("ctx", "head"),
        P("ctx", "head"),
        P("ctx", "head"),
        P("ctx", "head"),
        P("head"),
        P(),
        P(),
    )
    return jax.shard_map(
        body, mesh=mesh, in_specs=placed, out_specs=P("ctx", "head"), check_vma=False
    )
```

```python
import jax
import jax.numpy as jnp
from jax import lax
from jax.experimental import pallas as pl
from jax.experimental.pallas import tpu as pltpu
from jax.sharding import PartitionSpec as P

BLOCK = 128
EXTRA = 16
FAR = 1e9
OWN_EACH = 4
OUTGO_EACH = 4
FINISH_EACH = 8
F32 = jnp.float32
BF16 = jnp.bfloat16


def dot(a, b, contract):
    return lax.dot_general(a, b, ((contract[:1], contract[1:]), ((), ())), preferred_element_type=F32)


def triangle(upper):
    row = lax.broadcasted_iota(jnp.int32, (BLOCK, BLOCK), 0)
    column = lax.broadcasted_iota(jnp.int32, (BLOCK, BLOCK), 1)
    keep = row <= column if upper else column <= row
    return jnp.where(keep, 1.0, 0.0).astype(BF16)


def in_three(x):
    high = x.astype(BF16).astype(F32)
    middle = (x - high).astype(BF16).astype(F32)
    return high, middle, x - high - middle


def start_row(lengths):
    count = lengths.shape[1]
    row = lax.broadcasted_iota(jnp.int32, (count, BLOCK), 0)
    ahead = jnp.where(row < lax.broadcasted_iota(jnp.int32, (count, BLOCK), 1), 1.0, 0.0)
    wide = jnp.broadcast_to(lengths.astype(F32), (8, count))
    return lax.dot_general(
        wide, ahead, (((1,), (0,)), ((), ())), precision=lax.Precision.HIGHEST, preferred_element_type=F32
    )[:1]


def own_kernel(heads, blocks, each, packing, place, lengths, keys, values, decay, own, made, fates, sems):
    step = pl.program_id(0)
    per_head = made.shape[0] // heads
    pieces = BLOCK // per_head
    steps = blocks // each
    upper = triangle(True)
    starts = start_row(lengths[...])
    lane = lax.broadcasted_iota(jnp.int32, (1, BLOCK), 1).astype(F32)
    for inside in range(each):
        block = step * each + inside
        rows = slice(inside * BLOCK, (inside + 1) * BLOCK)
        base = (packing[place[0] * blocks + block] * BLOCK).astype(F32)
        logs = dot(decay[:, rows], upper, (1, 0))
        total = logs[:, BLOCK - 1 :]
        begun = jnp.where(starts <= base + (BLOCK - 1), starts, -FAR)
        started = jnp.max(begun, axis=1, keepdims=True)
        keep = jnp.exp(total - logs) * jnp.where(lane + base >= started, 1.0, 0.0)
        gate = jnp.exp(total) * jnp.where(started < base, 1.0, 0.0)
        to = pl.ds(pl.multiple_of(block * pieces, pieces), pieces)
        for head in range(heads):
            span = slice(head * BLOCK, (head + 1) * BLOCK)
            faded = keys[rows, span].T.astype(F32) * keep[head : head + 1, :]
            state = dot(faded.astype(BF16), values[rows, span], (1, 0)).astype(BF16)
            made[head * per_head : (head + 1) * per_head, to] = state.reshape(per_head, pieces, BLOCK)
            fates[head, pl.ds(block, 1), :] = jnp.broadcast_to(gate[head : head + 1, :], (1, BLOCK))

    def copy(at, start, size):
        part = (slice(None), pl.ds(start, size))
        return pltpu.make_async_copy(made.at[part], own.at[part], sems.at[at])

    span = each * pieces
    copy(step, pl.multiple_of(step * span, span), span).start()

    @pl.when(step == steps - 1)
    def _():
        at = lax.broadcasted_iota(jnp.int32, (EXTRA, BLOCK), 1)
        for head in range(heads):
            high, middle, low = in_three(fates[head])
            tile = jnp.where(at == 0, high, jnp.where(at == 1, middle, low)).astype(BF16)
            for piece in range(per_head):
                made[head * per_head + piece, blocks * pieces :] = tile
        copy(steps, blocks * pieces, EXTRA).start()
        for earlier in range(steps):
            copy(earlier, earlier * span, span).wait()
        copy(steps, blocks * pieces, EXTRA).wait()


def own_states(packing, place, lengths, keys, values, decay):
    rows, width = keys.shape
    heads = decay.shape[0]
    blocks = rows // BLOCK
    each = OWN_EACH
    devices = packing.shape[0] // blocks
    pieces = heads * BLOCK // devices
    shape = (devices, blocks * pieces + EXTRA, BLOCK)
    row_block = pl.BlockSpec((each * BLOCK, width), lambda b, *_: (b, 0))
    return pl.pallas_call(
        lambda *refs: own_kernel(heads, blocks, each, *refs),
        grid_spec=pltpu.PrefetchScalarGridSpec(
            num_scalar_prefetch=2,
            grid=(blocks // each,),
            in_specs=[
                pl.BlockSpec(lengths.shape, lambda b, *_: (0, 0)),
                row_block,
                row_block,
                pl.BlockSpec((heads, each * BLOCK), lambda b, *_: (0, b)),
            ],
            out_specs=pl.BlockSpec(memory_space=pl.ANY),
            scratch_shapes=[
                pltpu.VMEM(shape, BF16),
                pltpu.VMEM((heads, blocks, BLOCK), F32),
                pltpu.SemaphoreType.DMA((blocks // each + 1,)),
            ],
        ),
        out_shape=jax.ShapeDtypeStruct(shape, BF16),
        name="own",
    )(packing, place, lengths, keys, values, decay)


def intra_kernel(heads, packing, place, lengths, queries, keys, values, decay, intra, faded):
    block = pl.program_id(0)
    base = (packing[place[0] * pl.num_programs(0) + block] * BLOCK).astype(F32)
    along = dot(decay[...], triangle(True), (1, 0))
    down = dot(triangle(False), decay[...], (1, 1))
    row = lax.broadcasted_iota(jnp.int32, (BLOCK, BLOCK), 0)
    column = lax.broadcasted_iota(jnp.int32, (BLOCK, BLOCK), 1)
    begun = jnp.broadcast_to(start_row(lengths[...]), (BLOCK, BLOCK))
    begun = jnp.where(begun <= row.astype(F32) + base, begun, -FAR)
    started = jnp.max(begun, axis=1, keepdims=True)
    allowed = (column <= row) & (column.astype(F32) + base >= started)
    reach = jnp.exp(down) * jnp.where(started < base, 1.0, 0.0)
    for head in range(heads):
        span = slice(head * BLOCK, (head + 1) * BLOCK)
        query = queries[:, span]
        scores = dot(query, keys[:, span], (1, 1))
        gaps = jnp.minimum(down[:, head : head + 1] - along[head : head + 1, :], 0.0)
        weights = (scores * jnp.where(allowed, jnp.exp(gaps), 0.0)).astype(BF16)
        intra[:, span] = dot(weights, values[:, span], (1, 0))
        faded[:, span] = (query.astype(F32) * reach[:, head : head + 1]).astype(BF16)


def intra_pass(packing, place, lengths, queries, keys, values, decay):
    rows, width = queries.shape
    heads = decay.shape[0]
    row_block = pl.BlockSpec((BLOCK, width), lambda b, *_: (b, 0))
    return pl.pallas_call(
        lambda *refs: intra_kernel(heads, *refs),
        grid_spec=pltpu.PrefetchScalarGridSpec(
            num_scalar_prefetch=2,
            grid=(rows // BLOCK,),
            in_specs=[
                pl.BlockSpec(lengths.shape, lambda b, *_: (0, 0)),
                row_block,
                row_block,
                row_block,
                pl.BlockSpec((heads, BLOCK), lambda b, *_: (0, b)),
            ],
            out_specs=[row_block, row_block],
        ),
        out_shape=[
            jax.ShapeDtypeStruct((rows, width), F32),
            jax.ShapeDtypeStruct((rows, width), BF16),
        ],
        name="intra",
    )(packing, place, lengths, queries, keys, values, decay)


def scan_kernel(devices, blocks, order, own, prior, gates):
    each = own.shape[0] // devices
    parts = (each - 1) // blocks
    for device in range(devices):
        tile = own[(device + 1) * each - 1].astype(F32)
        gate = tile[:, 0:1] + tile[:, 1:2] + tile[:, 2:3]
        gates[device * blocks : (device + 1) * blocks, :] = jnp.broadcast_to(gate[:blocks], (blocks, BLOCK))

    def step(j, state):
        at = order[j]
        ahead = at * parts
        source = ahead + lax.shift_right_logical(at, blocks.bit_length() - 1)
        gate = gates[pl.ds(at, 1), :]
        after = []
        for part in range(parts):
            prior[ahead + part] = state[part].astype(BF16)
            after.append(gate * state[part] + own[source + part].astype(F32))
        return tuple(after)

    zero = jnp.zeros(own.shape[1:], F32)
    lax.fori_loop(0, devices * blocks, step, (zero,) * parts, unroll=16)


def scan_pass(order, own):
    devices, height, lanes = own.shape
    blocks = order.shape[0] // devices
    tiles = own.reshape(devices * height // EXTRA, EXTRA, lanes)
    vmem = pl.BlockSpec(memory_space=pltpu.VMEM)
    prior = pl.pallas_call(
        lambda *refs: scan_kernel(devices, blocks, *refs),
        in_specs=[pl.BlockSpec(memory_space=pltpu.SMEM), vmem],
        out_specs=vmem,
        out_shape=jax.ShapeDtypeStruct((tiles.shape[0] - devices, EXTRA, lanes), BF16),
        scratch_shapes=[pltpu.VMEM((devices * blocks, BLOCK), F32)],
        name="scan",
    )(order, tiles)
    return prior.reshape(devices, height - EXTRA, lanes)


def outgo_kernel(heads, blocks, each, packing, place, faded, intra, states, slots, made, sems):
    step = pl.program_id(0)
    per_head = states.shape[0] // heads
    pieces = BLOCK // per_head
    row = lax.broadcasted_iota(jnp.int32, (EXTRA, BLOCK), 0)

    def copy(block):
        owner = packing[place[0] * blocks + block] // blocks
        return pltpu.make_async_copy(made.at[block], slots.at[owner], sems.at[block])

    for inside in range(each):
        block = step * each + inside
        rows = slice(inside * BLOCK, (inside + 1) * BLOCK)
        sums = jnp.zeros((BLOCK, BLOCK), F32)
        for head in range(heads):
            span = slice(head * BLOCK, (head + 1) * BLOCK)
            state = states[
                head * per_head : (head + 1) * per_head, inside * pieces : (inside + 1) * pieces
            ].reshape(BLOCK, BLOCK)
            out = intra[rows, span] + dot(faded[rows, span], state, (1, 0))
            sums = sums + out * out
            made[block, span, :] = out.astype(BF16)
        high, middle, low = in_three(jnp.sum(sums.T, axis=0, keepdims=True))
        tile = jnp.where(row == 0, high, jnp.where(row == 1, middle, low))
        made[block, heads * BLOCK :, :] = tile.astype(BF16)
    for inside in range(each):
        copy(step * each + inside).start()

    @pl.when(step == pl.num_programs(0) - 1)
    def _():
        for block in range(blocks):
            copy(block).wait()


def outgo_pass(packing, place, faded, intra, states):
    rows, width = faded.shape
    blocks = rows // BLOCK
    devices, height, lanes = states.shape
    each = OUTGO_EACH
    heads = width // BLOCK
    row_block = pl.BlockSpec((each * BLOCK, width), lambda b, *_: (b, 0))
    return pl.pallas_call(
        lambda *refs: outgo_kernel(heads, blocks, each, *refs),
        grid_spec=pltpu.PrefetchScalarGridSpec(
            num_scalar_prefetch=2,
            grid=(blocks // each,),
            in_specs=[
                row_block,
                row_block,
                pl.BlockSpec((devices, height // blocks * each, lanes), lambda b, *_: (0, b, 0)),
            ],
            out_specs=pl.BlockSpec(memory_space=pl.ANY),
            scratch_shapes=[
                pltpu.VMEM((blocks, width + EXTRA, BLOCK), BF16),
                pltpu.SemaphoreType.DMA((blocks,)),
            ],
        ),
        out_shape=jax.ShapeDtypeStruct((devices, width + EXTRA, BLOCK), BF16),
        name="outgo",
    )(packing, place, faded, intra, states)


def squares_kernel(order, place, came, squares, tiles, sems):
    blocks, extra, _ = tiles.shape
    height = came.shape[1] - extra

    def copy(block):
        loader = order[place[0] * blocks + block] // blocks
        return pltpu.make_async_copy(came.at[loader, height:], tiles.at[block], sems.at[block])

    for block in range(blocks):
        copy(block).start()
    for block in range(blocks):
        copy(block).wait()
        tile = tiles[block].astype(F32)
        squares[block : block + 1, :] = tile[0:1, :] + tile[1:2, :] + tile[2:3, :]


def squares_pass(order, place, came):
    blocks = order.shape[0] // came.shape[0]
    smem = pl.BlockSpec(memory_space=pltpu.SMEM)
    return pl.pallas_call(
        squares_kernel,
        in_specs=[smem, smem, pl.BlockSpec(memory_space=pl.ANY)],
        out_specs=pl.BlockSpec(memory_space=pltpu.VMEM),
        out_shape=jax.ShapeDtypeStruct((blocks, BLOCK), F32),
        scratch_shapes=[
            pltpu.VMEM((blocks, EXTRA, BLOCK), BF16),
            pltpu.SemaphoreType.DMA((blocks,)),
        ],
        name="squares",
    )(order, place, came)


def finish_kernel(groups, each, order, place, *refs):
    squares, gain, parts, mixed = refs[:groups], refs[groups], refs[groups + 1 : -1], refs[-1]
    width = gain.shape[1]
    for inside in range(each):
        block = pl.ds(pl.program_id(0) * each + inside, 1)
        total = squares[0][block, :]
        for other in squares[1:]:
            total = total + other[block, :]
        scale = lax.rsqrt(total / (width * groups) + 1e-05)
        scale = jnp.broadcast_to(scale, (BLOCK, BLOCK)).T
        rows = slice(inside * BLOCK, (inside + 1) * BLOCK)
        for head in range(width // BLOCK):
            span = slice(head * BLOCK, (head + 1) * BLOCK)
            out = parts[inside][0, span, :].astype(F32) * scale * gain[:, span]
            mixed[rows, span] = out.astype(BF16)


def finish_pass(order, place, squares, gain, came):
    devices, height, lanes = came.shape
    blocks = order.shape[0] // devices
    width = gain.shape[1]
    each = FINISH_EACH

    def part(inside):
        def loader(b, order, place):
            return order[place[0] * blocks + b * each + inside] // blocks, 0, 0

        return pl.BlockSpec((1, width, lanes), loader)

    return pl.pallas_call(
        lambda *refs: finish_kernel(len(squares), each, *refs),
        grid_spec=pltpu.PrefetchScalarGridSpec(
            num_scalar_prefetch=2,
            grid=(blocks // each,),
            in_specs=[pl.BlockSpec((blocks, BLOCK), lambda b, *_: (0, 0))] * len(squares)
            + [pl.BlockSpec((1, width), lambda b, *_: (0, 0))]
            + [part(inside) for inside in range(each)],
            out_specs=pl.BlockSpec((each * BLOCK, width), lambda b, *_: (b, 0)),
        ),
        out_shape=jax.ShapeDtypeStruct((blocks * BLOCK, width), BF16),
        name="finish",
    )(order, place, *squares, gain, *[came] * each)


def swap(x, axis):
    return lax.all_to_all(x, axis, split_axis=0, concat_axis=0, tiled=True)


def body(queries, key_rows, value_rows, log_decay, norm_gain, doc_lengths, packing):
    mine = lax.axis_index("ctx").astype(jnp.int32)
    place = mine.reshape(1)
    decay = log_decay.T
    lengths = doc_lengths[None, :]

    own = swap(own_states(packing, place, lengths, key_rows, value_rows, decay), "ctx")
    intra, faded = intra_pass(packing, place, lengths, queries, key_rows, value_rows, decay)

    index = jnp.arange(packing.shape[0], dtype=jnp.int32)
    hit = (packing[None, :] == index[:, None]).astype(jnp.int32)
    order = jnp.sum(hit * index[None, :], axis=1)

    states = swap(scan_pass(order, own), "ctx")
    came = swap(outgo_pass(packing, place, faded, intra, states), "ctx")
    part = squares_pass(order, place, came)
    groups = lax.axis_size("head")
    squares = [part]
    for shift in range(1, groups):
        pairs = [(i, (i + shift) % groups) for i in range(groups)]
        squares.append(lax.ppermute(part, "head", pairs))
    return finish_pass(order, place, squares, norm_gain[None, :], came)


def solution(mesh):
    placed = (
        P("ctx", "head"),
        P("ctx", "head"),
        P("ctx", "head"),
        P("ctx", "head"),
        P("head"),
        P(),
        P(),
    )
    return jax.shard_map(
        body, mesh=mesh, in_specs=placed, out_specs=P("ctx", "head"), check_vma=False
    )
```

```python
import jax
import jax.numpy as jnp
from jax import lax
from jax.experimental import pallas as pl
from jax.experimental.pallas import tpu as pltpu
from jax.sharding import PartitionSpec as P

BLOCK = 128
EXTRA = 16
FAR = 1e9
OWN_EACH = 4
OUTGO_EACH = 4
FINISH_EACH = 8
F32 = jnp.float32
BF16 = jnp.bfloat16


def dot(a, b, contract):
    return lax.dot_general(a, b, ((contract[:1], contract[1:]), ((), ())), preferred_element_type=F32)


def triangle(upper):
    row = lax.broadcasted_iota(jnp.int32, (BLOCK, BLOCK), 0)
    column = lax.broadcasted_iota(jnp.int32, (BLOCK, BLOCK), 1)
    keep = row <= column if upper else column <= row
    return jnp.where(keep, 1.0, 0.0).astype(BF16)


def in_three(x):
    high = x.astype(BF16).astype(F32)
    middle = (x - high).astype(BF16).astype(F32)
    return high, middle, x - high - middle


def start_row(lengths):
    count = lengths.shape[1]
    row = lax.broadcasted_iota(jnp.int32, (count, BLOCK), 0)
    ahead = jnp.where(row < lax.broadcasted_iota(jnp.int32, (count, BLOCK), 1), 1.0, 0.0)
    wide = jnp.broadcast_to(lengths.astype(F32), (8, count))
    return lax.dot_general(
        wide, ahead, (((1,), (0,)), ((), ())), precision=lax.Precision.HIGHEST, preferred_element_type=F32
    )[:1]


def own_kernel(heads, blocks, each, packing, place, lengths, keys, values, decay, own, made, fates, sems):
    step = pl.program_id(0)
    per_head = made.shape[0] // heads
    pieces = BLOCK // per_head
    steps = blocks // each
    upper = triangle(True)
    starts = start_row(lengths[...])
    lane = lax.broadcasted_iota(jnp.int32, (1, BLOCK), 1).astype(F32)
    for inside in range(each):
        block = step * each + inside
        rows = slice(inside * BLOCK, (inside + 1) * BLOCK)
        base = (packing[place[0] * blocks + block] * BLOCK).astype(F32)
        logs = dot(decay[:, rows], upper, (1, 0))
        total = logs[:, BLOCK - 1 :]
        begun = jnp.where(starts <= base + (BLOCK - 1), starts, -FAR)
        started = jnp.max(begun, axis=1, keepdims=True)
        keep = jnp.exp(total - logs) * jnp.where(lane + base >= started, 1.0, 0.0)
        gate = jnp.exp(total) * jnp.where(started < base, 1.0, 0.0)
        to = pl.ds(pl.multiple_of(block * pieces, pieces), pieces)
        for head in range(heads):
            span = slice(head * BLOCK, (head + 1) * BLOCK)
            faded = keys[rows, span].T.astype(F32) * keep[head : head + 1, :]
            state = dot(faded.astype(BF16), values[rows, span], (1, 0)).astype(BF16)
            made[head * per_head : (head + 1) * per_head, to] = state.reshape(per_head, pieces, BLOCK)
            fates[head, pl.ds(block, 1), :] = jnp.broadcast_to(gate[head : head + 1, :], (1, BLOCK))

    def copy(at, start, size):
        part = (slice(None), pl.ds(start, size))
        return pltpu.make_async_copy(made.at[part], own.at[part], sems.at[at])

    span = each * pieces
    copy(step, pl.multiple_of(step * span, span), span).start()

    @pl.when(step == steps - 1)
    def _():
        at = lax.broadcasted_iota(jnp.int32, (EXTRA, BLOCK), 1)
        for head in range(heads):
            high, middle, low = in_three(fates[head])
            tile = jnp.where(at == 0, high, jnp.where(at == 1, middle, low)).astype(BF16)
            for piece in range(per_head):
                made[head * per_head + piece, blocks * pieces :] = tile
        copy(steps, blocks * pieces, EXTRA).start()
        for earlier in range(steps):
            copy(earlier, earlier * span, span).wait()
        copy(steps, blocks * pieces, EXTRA).wait()


def own_states(packing, place, lengths, keys, values, decay):
    rows, width = keys.shape
    heads = decay.shape[0]
    blocks = rows // BLOCK
    each = OWN_EACH
    devices = packing.shape[0] // blocks
    pieces = heads * BLOCK // devices
    shape = (devices, blocks * pieces + EXTRA, BLOCK)
    row_block = pl.BlockSpec((each * BLOCK, width), lambda b, *_: (b, 0))
    return pl.pallas_call(
        lambda *refs: own_kernel(heads, blocks, each, *refs),
        grid_spec=pltpu.PrefetchScalarGridSpec(
            num_scalar_prefetch=2,
            grid=(blocks // each,),
            in_specs=[
                pl.BlockSpec(lengths.shape, lambda b, *_: (0, 0)),
                row_block,
                row_block,
                pl.BlockSpec((heads, each * BLOCK), lambda b, *_: (0, b)),
            ],
            out_specs=pl.BlockSpec(memory_space=pl.ANY),
            scratch_shapes=[
                pltpu.VMEM(shape, BF16),
                pltpu.VMEM((heads, blocks, BLOCK), F32),
                pltpu.SemaphoreType.DMA((blocks // each + 1,)),
            ],
        ),
        out_shape=jax.ShapeDtypeStruct(shape, BF16),
        compiler_params=pltpu.CompilerParams(vmem_limit_bytes=14 * 2**20),
        name="own",
    )(packing, place, lengths, keys, values, decay)


def intra_kernel(heads, packing, place, lengths, queries, keys, values, decay, intra, faded):
    block = pl.program_id(0)
    base = (packing[place[0] * pl.num_programs(0) + block] * BLOCK).astype(F32)
    along = dot(decay[...], triangle(True), (1, 0))
    down = dot(triangle(False), decay[...], (1, 1))
    row = lax.broadcasted_iota(jnp.int32, (BLOCK, BLOCK), 0)
    column = lax.broadcasted_iota(jnp.int32, (BLOCK, BLOCK), 1)
    begun = jnp.broadcast_to(start_row(lengths[...]), (BLOCK, BLOCK))
    begun = jnp.where(begun <= row.astype(F32) + base, begun, -FAR)
    started = jnp.max(begun, axis=1, keepdims=True)
    allowed = (column <= row) & (column.astype(F32) + base >= started)
    reach = jnp.exp(down) * jnp.where(started < base, 1.0, 0.0)
    for head in range(heads):
        span = slice(head * BLOCK, (head + 1) * BLOCK)
        query = queries[:, span]
        scores = dot(query, keys[:, span], (1, 1))
        gaps = jnp.minimum(down[:, head : head + 1] - along[head : head + 1, :], 0.0)
        weights = (scores * jnp.where(allowed, jnp.exp(gaps), 0.0)).astype(BF16)
        intra[:, span] = dot(weights, values[:, span], (1, 0))
        faded[:, span] = (query.astype(F32) * reach[:, head : head + 1]).astype(BF16)


def intra_pass(packing, place, lengths, queries, keys, values, decay):
    rows, width = queries.shape
    heads = decay.shape[0]
    row_block = pl.BlockSpec((BLOCK, width), lambda b, *_: (b, 0))
    return pl.pallas_call(
        lambda *refs: intra_kernel(heads, *refs),
        grid_spec=pltpu.PrefetchScalarGridSpec(
            num_scalar_prefetch=2,
            grid=(rows // BLOCK,),
            in_specs=[
                pl.BlockSpec(lengths.shape, lambda b, *_: (0, 0)),
                row_block,
                row_block,
                row_block,
                pl.BlockSpec((heads, BLOCK), lambda b, *_: (0, b)),
            ],
            out_specs=[row_block, row_block],
        ),
        out_shape=[
            jax.ShapeDtypeStruct((rows, width), F32),
            jax.ShapeDtypeStruct((rows, width), BF16),
        ],
        name="intra",
    )(packing, place, lengths, queries, keys, values, decay)


def scan_kernel(devices, blocks, order, own, prior, gates):
    each = own.shape[0] // devices
    parts = (each - 1) // blocks
    for device in range(devices):
        tile = own[(device + 1) * each - 1].astype(F32)
        gate = tile[:, 0:1] + tile[:, 1:2] + tile[:, 2:3]
        gates[device * blocks : (device + 1) * blocks, :] = jnp.broadcast_to(gate[:blocks], (blocks, BLOCK))

    def step(j, state):
        at = order[j]
        ahead = at * parts
        source = ahead + lax.shift_right_logical(at, blocks.bit_length() - 1)
        gate = gates[pl.ds(at, 1), :]
        after = []
        for part in range(parts):
            prior[ahead + part] = state[part].astype(BF16)
            after.append(gate * state[part] + own[source + part].astype(F32))
        return tuple(after)

    zero = jnp.zeros(own.shape[1:], F32)
    lax.fori_loop(0, devices * blocks, step, (zero,) * parts, unroll=16)


def scan_pass(order, own):
    devices, height, lanes = own.shape
    blocks = order.shape[0] // devices
    tiles = own.reshape(devices * height // EXTRA, EXTRA, lanes)
    vmem = pl.BlockSpec(memory_space=pltpu.VMEM)
    prior = pl.pallas_call(
        lambda *refs: scan_kernel(devices, blocks, *refs),
        in_specs=[pl.BlockSpec(memory_space=pltpu.SMEM), vmem],
        out_specs=vmem,
        out_shape=jax.ShapeDtypeStruct((tiles.shape[0] - devices, EXTRA, lanes), BF16),
        scratch_shapes=[pltpu.VMEM((devices * blocks, BLOCK), F32)],
        compiler_params=pltpu.CompilerParams(vmem_limit_bytes=20 * 2**20),
        name="scan",
    )(order, tiles)
    return prior.reshape(devices, height - EXTRA, lanes)


def outgo_kernel(heads, blocks, each, packing, place, faded, intra, states, slots, made, sems):
    step = pl.program_id(0)
    per_head = states.shape[0] // heads
    pieces = BLOCK // per_head
    row = lax.broadcasted_iota(jnp.int32, (EXTRA, BLOCK), 0)

    def copy(block):
        owner = packing[place[0] * blocks + block] // blocks
        return pltpu.make_async_copy(made.at[block], slots.at[owner], sems.at[block])

    for inside in range(each):
        block = step * each + inside
        rows = slice(inside * BLOCK, (inside + 1) * BLOCK)
        sums = jnp.zeros((BLOCK, BLOCK), F32)
        for head in range(heads):
            span = slice(head * BLOCK, (head + 1) * BLOCK)
            state = states[
                head * per_head : (head + 1) * per_head, inside * pieces : (inside + 1) * pieces
            ].reshape(BLOCK, BLOCK)
            out = intra[rows, span] + dot(faded[rows, span], state, (1, 0))
            sums = sums + out * out
            made[block, span, :] = out.astype(BF16)
        high, middle, low = in_three(jnp.sum(sums.T, axis=0, keepdims=True))
        tile = jnp.where(row == 0, high, jnp.where(row == 1, middle, low))
        made[block, heads * BLOCK :, :] = tile.astype(BF16)
    for inside in range(each):
        copy(step * each + inside).start()

    @pl.when(step == pl.num_programs(0) - 1)
    def _():
        for block in range(blocks):
            copy(block).wait()


def outgo_pass(packing, place, faded, intra, states):
    rows, width = faded.shape
    blocks = rows // BLOCK
    devices, height, lanes = states.shape
    each = OUTGO_EACH
    heads = width // BLOCK
    row_block = pl.BlockSpec((each * BLOCK, width), lambda b, *_: (b, 0))
    return pl.pallas_call(
        lambda *refs: outgo_kernel(heads, blocks, each, *refs),
        grid_spec=pltpu.PrefetchScalarGridSpec(
            num_scalar_prefetch=2,
            grid=(blocks // each,),
            in_specs=[
                row_block,
                row_block,
                pl.BlockSpec((devices, height // blocks * each, lanes), lambda b, *_: (0, b, 0)),
            ],
            out_specs=pl.BlockSpec(memory_space=pl.ANY),
            scratch_shapes=[
                pltpu.VMEM((blocks, width + EXTRA, BLOCK), BF16),
                pltpu.SemaphoreType.DMA((blocks,)),
            ],
        ),
        out_shape=jax.ShapeDtypeStruct((devices, width + EXTRA, BLOCK), BF16),
        compiler_params=pltpu.CompilerParams(vmem_limit_bytes=18 * 2**20),
        name="outgo",
    )(packing, place, faded, intra, states)


def squares_kernel(order, place, came, squares, tiles, sems):
    blocks, extra, _ = tiles.shape
    height = came.shape[1] - extra

    def copy(block):
        loader = order[place[0] * blocks + block] // blocks
        return pltpu.make_async_copy(came.at[loader, height:], tiles.at[block], sems.at[block])

    for block in range(blocks):
        copy(block).start()
    for block in range(blocks):
        copy(block).wait()
        tile = tiles[block].astype(F32)
        squares[block : block + 1, :] = tile[0:1, :] + tile[1:2, :] + tile[2:3, :]


def squares_pass(order, place, came):
    blocks = order.shape[0] // came.shape[0]
    smem = pl.BlockSpec(memory_space=pltpu.SMEM)
    return pl.pallas_call(
        squares_kernel,
        in_specs=[smem, smem, pl.BlockSpec(memory_space=pl.ANY)],
        out_specs=pl.BlockSpec(memory_space=pltpu.VMEM),
        out_shape=jax.ShapeDtypeStruct((blocks, BLOCK), F32),
        scratch_shapes=[
            pltpu.VMEM((blocks, EXTRA, BLOCK), BF16),
            pltpu.SemaphoreType.DMA((blocks,)),
        ],
        compiler_params=pltpu.CompilerParams(vmem_limit_bytes=2 * 2**20),
        name="squares",
    )(order, place, came)


def finish_kernel(groups, each, order, place, *refs):
    squares, gain, parts, mixed = refs[:groups], refs[groups], refs[groups + 1 : -1], refs[-1]
    width = gain.shape[1]
    for inside in range(each):
        block = pl.ds(pl.program_id(0) * each + inside, 1)
        total = squares[0][block, :]
        for other in squares[1:]:
            total = total + other[block, :]
        scale = lax.rsqrt(total / (width * groups) + 1e-05)
        scale = jnp.broadcast_to(scale, (BLOCK, BLOCK)).T
        rows = slice(inside * BLOCK, (inside + 1) * BLOCK)
        for head in range(width // BLOCK):
            span = slice(head * BLOCK, (head + 1) * BLOCK)
            out = parts[inside][0, span, :].astype(F32) * scale * gain[:, span]
            mixed[rows, span] = out.astype(BF16)


def finish_pass(order, place, squares, gain, came):
    devices, height, lanes = came.shape
    blocks = order.shape[0] // devices
    width = gain.shape[1]
    each = FINISH_EACH

    def part(inside):
        def loader(b, order, place):
            return order[place[0] * blocks + b * each + inside] // blocks, 0, 0

        return pl.BlockSpec((1, width, lanes), loader)

    return pl.pallas_call(
        lambda *refs: finish_kernel(len(squares), each, *refs),
        grid_spec=pltpu.PrefetchScalarGridSpec(
            num_scalar_prefetch=2,
            grid=(blocks // each,),
            in_specs=[pl.BlockSpec((blocks, BLOCK), lambda b, *_: (0, 0))] * len(squares)
            + [pl.BlockSpec((1, width), lambda b, *_: (0, 0))]
            + [part(inside) for inside in range(each)],
            out_specs=pl.BlockSpec((each * BLOCK, width), lambda b, *_: (b, 0)),
        ),
        out_shape=jax.ShapeDtypeStruct((blocks * BLOCK, width), BF16),
        compiler_params=pltpu.CompilerParams(vmem_limit_bytes=14 * 2**20),
        name="finish",
    )(order, place, *squares, gain, *[came] * each)


def swap(x, axis):
    return lax.all_to_all(x, axis, split_axis=0, concat_axis=0, tiled=True)


def body(queries, key_rows, value_rows, log_decay, norm_gain, doc_lengths, packing):
    mine = lax.axis_index("ctx").astype(jnp.int32)
    place = mine.reshape(1)
    decay = log_decay.T
    lengths = doc_lengths[None, :]

    index = jnp.arange(packing.shape[0], dtype=jnp.int32)
    hit = (packing[None, :] == index[:, None]).astype(jnp.int32)
    order = jnp.sum(hit * index[None, :], axis=1)

    packing, order = lax.optimization_barrier((packing, order))
    held = [pltpu.with_memory_space_constraint(x, pltpu.HBM) for x in (key_rows, value_rows)]
    own = swap(own_states(packing, place, lengths, *held, decay), "ctx")
    intra, faded = intra_pass(packing, place, lengths, queries, key_rows, value_rows, decay)

    states = swap(scan_pass(order, own), "ctx")
    faded, intra = (pltpu.with_memory_space_constraint(x, pltpu.HBM) for x in (faded, intra))
    came = swap(outgo_pass(packing, place, faded, intra, states), "ctx")
    part = squares_pass(order, place, came)
    groups = lax.axis_size("head")
    squares = [part]
    for shift in range(1, groups):
        pairs = [(i, (i + shift) % groups) for i in range(groups)]
        squares.append(lax.ppermute(part, "head", pairs))
    return finish_pass(order, place, squares, norm_gain[None, :], came)


def solution(mesh):
    placed = (
        P("ctx", "head"),
        P("ctx", "head"),
        P("ctx", "head"),
        P("ctx", "head"),
        P("head"),
        P(),
        P(),
    )
    return jax.shard_map(
        body, mesh=mesh, in_specs=placed, out_specs=P("ctx", "head"), check_vma=False
    )
```

```python
import jax
import jax.numpy as jnp
from jax import lax
from jax.experimental import pallas as pl
from jax.experimental.pallas import tpu as pltpu
from jax.sharding import PartitionSpec as P

BLOCK = 128
EXTRA = 16
FAR = 1e9
OWN_EACH = 4
OUTGO_EACH = 4
FINISH_EACH = 8
F32 = jnp.float32
BF16 = jnp.bfloat16


def dot(a, b, contract):
    return lax.dot_general(a, b, ((contract[:1], contract[1:]), ((), ())), preferred_element_type=F32)


def triangle(upper):
    row = lax.broadcasted_iota(jnp.int32, (BLOCK, BLOCK), 0)
    column = lax.broadcasted_iota(jnp.int32, (BLOCK, BLOCK), 1)
    keep = row <= column if upper else column <= row
    return jnp.where(keep, 1.0, 0.0).astype(BF16)


def in_three(x):
    high = x.astype(BF16).astype(F32)
    middle = (x - high).astype(BF16).astype(F32)
    return high, middle, x - high - middle


def start_row(lengths):
    count = lengths.shape[1]
    row = lax.broadcasted_iota(jnp.int32, (count, BLOCK), 0)
    ahead = jnp.where(row < lax.broadcasted_iota(jnp.int32, (count, BLOCK), 1), 1.0, 0.0)
    wide = jnp.broadcast_to(lengths.astype(F32), (8, count))
    return lax.dot_general(
        wide, ahead, (((1,), (0,)), ((), ())), precision=lax.Precision.HIGHEST, preferred_element_type=F32
    )[:1]


def own_kernel(heads, blocks, each, packing, place, lengths, keys, values, decay, own, made, fates, sems):
    step = pl.program_id(0)
    per_head = made.shape[0] // heads
    pieces = BLOCK // per_head
    steps = blocks // each
    upper = triangle(True)
    starts = start_row(lengths[...])
    lane = lax.broadcasted_iota(jnp.int32, (1, BLOCK), 1).astype(F32)
    for inside in range(each):
        block = step * each + inside
        rows = slice(inside * BLOCK, (inside + 1) * BLOCK)
        base = (packing[place[0] * blocks + block] * BLOCK).astype(F32)
        logs = dot(decay[:, rows], upper, (1, 0))
        total = logs[:, BLOCK - 1 :]
        begun = jnp.where(starts <= base + (BLOCK - 1), starts, -FAR)
        started = jnp.max(begun, axis=1, keepdims=True)
        keep = jnp.exp(total - logs) * jnp.where(lane + base >= started, 1.0, 0.0)
        gate = jnp.exp(total) * jnp.where(started < base, 1.0, 0.0)
        to = pl.ds(pl.multiple_of(block * pieces, pieces), pieces)
        for head in range(heads):
            span = slice(head * BLOCK, (head + 1) * BLOCK)
            faded = keys[rows, span].T.astype(F32) * keep[head : head + 1, :]
            state = dot(faded.astype(BF16), values[rows, span], (1, 0)).astype(BF16)
            made[head * per_head : (head + 1) * per_head, to] = state.reshape(per_head, pieces, BLOCK)
            fates[head, pl.ds(block, 1), :] = jnp.broadcast_to(gate[head : head + 1, :], (1, BLOCK))

    def copy(at, start, size):
        part = (slice(None), pl.ds(start, size))
        return pltpu.make_async_copy(made.at[part], own.at[part], sems.at[at])

    span = each * pieces
    copy(step, pl.multiple_of(step * span, span), span).start()

    @pl.when(step == steps - 1)
    def _():
        at = lax.broadcasted_iota(jnp.int32, (EXTRA, BLOCK), 1)
        for head in range(heads):
            high, middle, low = in_three(fates[head])
            tile = jnp.where(at == 0, high, jnp.where(at == 1, middle, low)).astype(BF16)
            for piece in range(per_head):
                made[head * per_head + piece, blocks * pieces :] = tile
        copy(steps, blocks * pieces, EXTRA).start()
        for earlier in range(steps):
            copy(earlier, earlier * span, span).wait()
        copy(steps, blocks * pieces, EXTRA).wait()


def own_states(packing, place, lengths, keys, values, decay):
    rows, width = keys.shape
    heads = decay.shape[0]
    blocks = rows // BLOCK
    each = OWN_EACH
    devices = packing.shape[0] // blocks
    pieces = heads * BLOCK // devices
    shape = (devices, blocks * pieces + EXTRA, BLOCK)
    row_block = pl.BlockSpec((each * BLOCK, width), lambda b, *_: (b, 0))
    return pl.pallas_call(
        lambda *refs: own_kernel(heads, blocks, each, *refs),
        grid_spec=pltpu.PrefetchScalarGridSpec(
            num_scalar_prefetch=2,
            grid=(blocks // each,),
            in_specs=[
                pl.BlockSpec(lengths.shape, lambda b, *_: (0, 0)),
                row_block,
                row_block,
                pl.BlockSpec((heads, each * BLOCK), lambda b, *_: (0, b)),
            ],
            out_specs=pl.BlockSpec(memory_space=pl.ANY),
            scratch_shapes=[
                pltpu.VMEM(shape, BF16),
                pltpu.VMEM((heads, blocks, BLOCK), F32),
                pltpu.SemaphoreType.DMA((blocks // each + 1,)),
            ],
        ),
        out_shape=jax.ShapeDtypeStruct(shape, BF16),
        name="own",
    )(packing, place, lengths, keys, values, decay)


def intra_kernel(heads, packing, place, lengths, queries, keys, values, decay, intra, faded):
    block = pl.program_id(0)
    base = (packing[place[0] * pl.num_programs(0) + block] * BLOCK).astype(F32)
    along = dot(decay[...], triangle(True), (1, 0))
    down = dot(triangle(False), decay[...], (1, 1))
    row = lax.broadcasted_iota(jnp.int32, (BLOCK, BLOCK), 0)
    column = lax.broadcasted_iota(jnp.int32, (BLOCK, BLOCK), 1)
    begun = jnp.broadcast_to(start_row(lengths[...]), (BLOCK, BLOCK))
    begun = jnp.where(begun <= row.astype(F32) + base, begun, -FAR)
    started = jnp.max(begun, axis=1, keepdims=True)
    allowed = (column <= row) & (column.astype(F32) + base >= started)
    reach = jnp.exp(down) * jnp.where(started < base, 1.0, 0.0)
    for head in range(heads):
        span = slice(head * BLOCK, (head + 1) * BLOCK)
        query = queries[:, span]
        scores = dot(query, keys[:, span], (1, 1))
        gaps = jnp.minimum(down[:, head : head + 1] - along[head : head + 1, :], 0.0)
        weights = (scores * jnp.where(allowed, jnp.exp(gaps), 0.0)).astype(BF16)
        intra[:, span] = dot(weights, values[:, span], (1, 0))
        faded[:, span] = (query.astype(F32) * reach[:, head : head + 1]).astype(BF16)


def intra_pass(packing, place, lengths, queries, keys, values, decay):
    rows, width = queries.shape
    heads = decay.shape[0]
    row_block = pl.BlockSpec((BLOCK, width), lambda b, *_: (b, 0))
    return pl.pallas_call(
        lambda *refs: intra_kernel(heads, *refs),
        grid_spec=pltpu.PrefetchScalarGridSpec(
            num_scalar_prefetch=2,
            grid=(rows // BLOCK,),
            in_specs=[
                pl.BlockSpec(lengths.shape, lambda b, *_: (0, 0)),
                row_block,
                row_block,
                row_block,
                pl.BlockSpec((heads, BLOCK), lambda b, *_: (0, b)),
            ],
            out_specs=[row_block, row_block],
        ),
        out_shape=[
            jax.ShapeDtypeStruct((rows, width), F32),
            jax.ShapeDtypeStruct((rows, width), BF16),
        ],
        name="intra",
    )(packing, place, lengths, queries, keys, values, decay)


def scan_kernel(devices, blocks, order, own, prior, gates):
    each = own.shape[0] // devices
    parts = (each - 1) // blocks
    for device in range(devices):
        tile = own[(device + 1) * each - 1].astype(F32)
        gate = tile[:, 0:1] + tile[:, 1:2] + tile[:, 2:3]
        gates[device * blocks : (device + 1) * blocks, :] = jnp.broadcast_to(gate[:blocks], (blocks, BLOCK))

    def step(j, state):
        at = order[j]
        ahead = at * parts
        source = ahead + lax.shift_right_logical(at, blocks.bit_length() - 1)
        gate = gates[pl.ds(at, 1), :]
        after = []
        for part in range(parts):
            prior[ahead + part] = state[part].astype(BF16)
            after.append(gate * state[part] + own[source + part].astype(F32))
        return tuple(after)

    zero = jnp.zeros(own.shape[1:], F32)
    lax.fori_loop(0, devices * blocks, step, (zero,) * parts, unroll=16)


def scan_pass(order, own):
    devices, height, lanes = own.shape
    blocks = order.shape[0] // devices
    tiles = own.reshape(devices * height // EXTRA, EXTRA, lanes)
    vmem = pl.BlockSpec(memory_space=pltpu.VMEM)
    prior = pl.pallas_call(
        lambda *refs: scan_kernel(devices, blocks, *refs),
        in_specs=[pl.BlockSpec(memory_space=pltpu.SMEM), vmem],
        out_specs=vmem,
        out_shape=jax.ShapeDtypeStruct((tiles.shape[0] - devices, EXTRA, lanes), BF16),
        scratch_shapes=[pltpu.VMEM((devices * blocks, BLOCK), F32)],
        compiler_params=pltpu.CompilerParams(vmem_limit_bytes=20 * 2**20),
        name="scan",
    )(order, tiles)
    return prior.reshape(devices, height - EXTRA, lanes)


def outgo_kernel(heads, blocks, each, packing, place, faded, intra, states, slots, made, sems):
    step = pl.program_id(0)
    per_head = states.shape[0] // heads
    pieces = BLOCK // per_head
    row = lax.broadcasted_iota(jnp.int32, (EXTRA, BLOCK), 0)

    def copy(block):
        owner = packing[place[0] * blocks + block] // blocks
        return pltpu.make_async_copy(made.at[block], slots.at[owner], sems.at[block])

    for inside in range(each):
        block = step * each + inside
        rows = slice(inside * BLOCK, (inside + 1) * BLOCK)
        sums = jnp.zeros((BLOCK, BLOCK), F32)
        for head in range(heads):
            span = slice(head * BLOCK, (head + 1) * BLOCK)
            state = states[
                head * per_head : (head + 1) * per_head, inside * pieces : (inside + 1) * pieces
            ].reshape(BLOCK, BLOCK)
            out = intra[rows, span] + dot(faded[rows, span], state, (1, 0))
            sums = sums + out * out
            made[block, span, :] = out.astype(BF16)
        high, middle, low = in_three(jnp.sum(sums.T, axis=0, keepdims=True))
        tile = jnp.where(row == 0, high, jnp.where(row == 1, middle, low))
        made[block, heads * BLOCK :, :] = tile.astype(BF16)
    for inside in range(each):
        copy(step * each + inside).start()

    @pl.when(step == pl.num_programs(0) - 1)
    def _():
        for block in range(blocks):
            copy(block).wait()


def outgo_pass(packing, place, faded, intra, states):
    rows, width = faded.shape
    blocks = rows // BLOCK
    devices, height, lanes = states.shape
    each = OUTGO_EACH
    heads = width // BLOCK
    row_block = pl.BlockSpec((each * BLOCK, width), lambda b, *_: (b, 0))
    return pl.pallas_call(
        lambda *refs: outgo_kernel(heads, blocks, each, *refs),
        grid_spec=pltpu.PrefetchScalarGridSpec(
            num_scalar_prefetch=2,
            grid=(blocks // each,),
            in_specs=[
                row_block,
                row_block,
                pl.BlockSpec((devices, height // blocks * each, lanes), lambda b, *_: (0, b, 0)),
            ],
            out_specs=pl.BlockSpec(memory_space=pl.ANY),
            scratch_shapes=[
                pltpu.VMEM((blocks, width + EXTRA, BLOCK), BF16),
                pltpu.SemaphoreType.DMA((blocks,)),
            ],
        ),
        out_shape=jax.ShapeDtypeStruct((devices, width + EXTRA, BLOCK), BF16),
        compiler_params=pltpu.CompilerParams(vmem_limit_bytes=18 * 2**20),
        name="outgo",
    )(packing, place, faded, intra, states)


def squares_kernel(order, place, came, squares, tiles, sems):
    blocks, extra, _ = tiles.shape
    height = came.shape[1] - extra

    def copy(block):
        loader = order[place[0] * blocks + block] // blocks
        return pltpu.make_async_copy(came.at[loader, height:], tiles.at[block], sems.at[block])

    for block in range(blocks):
        copy(block).start()
    for block in range(blocks):
        copy(block).wait()
        tile = tiles[block].astype(F32)
        squares[block : block + 1, :] = tile[0:1, :] + tile[1:2, :] + tile[2:3, :]


def squares_pass(order, place, came):
    blocks = order.shape[0] // came.shape[0]
    smem = pl.BlockSpec(memory_space=pltpu.SMEM)
    return pl.pallas_call(
        squares_kernel,
        in_specs=[smem, smem, pl.BlockSpec(memory_space=pl.ANY)],
        out_specs=pl.BlockSpec(memory_space=pltpu.VMEM),
        out_shape=jax.ShapeDtypeStruct((blocks, BLOCK), F32),
        scratch_shapes=[
            pltpu.VMEM((blocks, EXTRA, BLOCK), BF16),
            pltpu.SemaphoreType.DMA((blocks,)),
        ],
        compiler_params=pltpu.CompilerParams(vmem_limit_bytes=2 * 2**20),
        name="squares",
    )(order, place, came)


def finish_kernel(groups, each, order, place, *refs):
    squares, gain, parts, mixed = refs[:groups], refs[groups], refs[groups + 1 : -1], refs[-1]
    width = gain.shape[1]
    for inside in range(each):
        block = pl.ds(pl.program_id(0) * each + inside, 1)
        total = squares[0][block, :]
        for other in squares[1:]:
            total = total + other[block, :]
        scale = lax.rsqrt(total / (width * groups) + 1e-05)
        scale = jnp.broadcast_to(scale, (BLOCK, BLOCK)).T
        rows = slice(inside * BLOCK, (inside + 1) * BLOCK)
        for head in range(width // BLOCK):
            span = slice(head * BLOCK, (head + 1) * BLOCK)
            out = parts[inside][0, span, :].astype(F32) * scale * gain[:, span]
            mixed[rows, span] = out.astype(BF16)


def finish_pass(order, place, squares, gain, came):
    devices, height, lanes = came.shape
    blocks = order.shape[0] // devices
    width = gain.shape[1]
    each = FINISH_EACH

    def part(inside):
        def loader(b, order, place):
            return order[place[0] * blocks + b * each + inside] // blocks, 0, 0

        return pl.BlockSpec((1, width, lanes), loader)

    return pl.pallas_call(
        lambda *refs: finish_kernel(len(squares), each, *refs),
        grid_spec=pltpu.PrefetchScalarGridSpec(
            num_scalar_prefetch=2,
            grid=(blocks // each,),
            in_specs=[pl.BlockSpec((blocks, BLOCK), lambda b, *_: (0, 0))] * len(squares)
            + [pl.BlockSpec((1, width), lambda b, *_: (0, 0))]
            + [part(inside) for inside in range(each)],
            out_specs=pl.BlockSpec((each * BLOCK, width), lambda b, *_: (b, 0)),
        ),
        out_shape=jax.ShapeDtypeStruct((blocks * BLOCK, width), BF16),
        compiler_params=pltpu.CompilerParams(vmem_limit_bytes=14 * 2**20),
        name="finish",
    )(order, place, *squares, gain, *[came] * each)


def swap(x, axis):
    return lax.all_to_all(x, axis, split_axis=0, concat_axis=0, tiled=True)


def body(queries, key_rows, value_rows, log_decay, norm_gain, doc_lengths, packing):
    mine = lax.axis_index("ctx").astype(jnp.int32)
    place = mine.reshape(1)
    decay = log_decay.T
    lengths = doc_lengths[None, :]

    index = jnp.arange(packing.shape[0], dtype=jnp.int32)
    hit = (packing[None, :] == index[:, None]).astype(jnp.int32)
    order = jnp.sum(hit * index[None, :], axis=1)

    own = swap(own_states(packing, place, lengths, key_rows, value_rows, decay), "ctx")
    intra, faded = intra_pass(packing, place, lengths, queries, key_rows, value_rows, decay)

    own, order, intra, faded = lax.optimization_barrier((own, order, intra, faded))
    states = swap(scan_pass(order, own), "ctx")
    came = swap(outgo_pass(packing, place, faded, intra, states), "ctx")
    part = squares_pass(order, place, came)
    groups = lax.axis_size("head")
    squares = [part]
    for shift in range(1, groups):
        pairs = [(i, (i + shift) % groups) for i in range(groups)]
        squares.append(lax.ppermute(part, "head", pairs))
    return finish_pass(order, place, squares, norm_gain[None, :], came)


def solution(mesh):
    placed = (
        P("ctx", "head"),
        P("ctx", "head"),
        P("ctx", "head"),
        P("ctx", "head"),
        P("head"),
        P(),
        P(),
    )
    return jax.shard_map(
        body, mesh=mesh, in_specs=placed, out_specs=P("ctx", "head"), check_vma=False
    )
```

```python
import jax
import jax.numpy as jnp
from jax import lax
from jax.experimental import pallas as pl
from jax.experimental.pallas import tpu as pltpu
from jax.sharding import PartitionSpec as P

BLOCK = 128
EXTRA = 16
TAIL = 8
FAR = 1e9
OWN_EACH = 8
OUTGO_EACH = 4
FINISH_EACH = 8
F32 = jnp.float32
BF16 = jnp.bfloat16


def dot(a, b, contract):
    return lax.dot_general(a, b, ((contract[:1], contract[1:]), ((), ())), preferred_element_type=F32)


def triangle(upper):
    row = lax.broadcasted_iota(jnp.int32, (BLOCK, BLOCK), 0)
    column = lax.broadcasted_iota(jnp.int32, (BLOCK, BLOCK), 1)
    keep = row <= column if upper else column <= row
    return jnp.where(keep, 1.0, 0.0).astype(BF16)


def in_three(x):
    high = x.astype(BF16).astype(F32)
    middle = (x - high).astype(BF16).astype(F32)
    return high, middle, x - high - middle


def start_row(lengths):
    count = lengths.shape[1]
    row = lax.broadcasted_iota(jnp.int32, (count, BLOCK), 0)
    ahead = jnp.where(row < lax.broadcasted_iota(jnp.int32, (count, BLOCK), 1), 1.0, 0.0)
    wide = jnp.broadcast_to(lengths.astype(F32), (8, count))
    return lax.dot_general(
        wide, ahead, (((1,), (0,)), ((), ())), precision=lax.Precision.HIGHEST, preferred_element_type=F32
    )[:1]


def own_kernel(heads, blocks, each, packing, place, lengths, keys, values, decay, own, made, fates, faded, sems):
    step = pl.program_id(0)
    per_head = made.shape[0] // heads
    pieces = BLOCK // per_head
    steps = blocks // each
    upper = triangle(True)
    starts = start_row(lengths[...])
    lane = lax.broadcasted_iota(jnp.int32, (1, BLOCK), 1).astype(F32)
    keeps = []
    for inside in range(each):
        block = step * each + inside
        rows = slice(inside * BLOCK, (inside + 1) * BLOCK)
        base = (packing[place[0] * blocks + block] * BLOCK).astype(F32)
        logs = dot(decay[:, rows], upper, (1, 0))
        total = logs[:, BLOCK - 1 :]
        begun = jnp.where(starts <= base + (BLOCK - 1), starts, -FAR)
        started = jnp.max(begun, axis=1, keepdims=True)
        keeps.append(jnp.exp(total - logs) * jnp.where(lane + base >= started, 1.0, 0.0))
        gate = jnp.exp(total) * jnp.where(started < base, 1.0, 0.0)
        for head in range(heads):
            fates[head, pl.ds(block, 1), :] = jnp.broadcast_to(gate[head : head + 1, :], (1, BLOCK))

    def fade(inside, head):
        rows = slice(inside * BLOCK, (inside + 1) * BLOCK)
        span = slice(head * BLOCK, (head + 1) * BLOCK)
        turned = keys[rows, span].T.astype(F32) * keeps[inside][head : head + 1, :]
        faded[inside, head] = turned.astype(BF16)

    def multiply(inside, head):
        rows = slice(inside * BLOCK, (inside + 1) * BLOCK)
        span = slice(head * BLOCK, (head + 1) * BLOCK)
        state = dot(faded[inside, head], values[rows, span], (1, 0)).astype(BF16)
        to = pl.ds(pl.multiple_of((step * each + inside) * pieces, pieces), pieces)
        made[head * per_head : (head + 1) * per_head, to] = state.reshape(per_head, pieces, BLOCK)

    for inside in range(each + 1):
        for head in range(heads):
            if inside < each:
                fade(inside, head)
            if inside:
                multiply(inside - 1, head)

    def copy(at, start, size):
        part = (slice(None), pl.ds(start, size))
        return pltpu.make_async_copy(made.at[part], own.at[part], sems.at[at])

    span = each * pieces
    copy(step, pl.multiple_of(step * span, span), span).start()

    @pl.when(step == steps - 1)
    def _():
        at = lax.broadcasted_iota(jnp.int32, (EXTRA, BLOCK), 1)
        for head in range(heads):
            high, middle, low = in_three(fates[head])
            tile = jnp.where(at == 0, high, jnp.where(at == 1, middle, low)).astype(BF16)
            for piece in range(per_head):
                made[head * per_head + piece, blocks * pieces :] = tile
        copy(steps, blocks * pieces, EXTRA).start()
        for earlier in range(steps):
            copy(earlier, earlier * span, span).wait()
        copy(steps, blocks * pieces, EXTRA).wait()


def own_states(packing, place, lengths, keys, values, decay):
    rows, width = keys.shape
    heads = decay.shape[0]
    blocks = rows // BLOCK
    each = OWN_EACH
    devices = packing.shape[0] // blocks
    pieces = heads * BLOCK // devices
    shape = (devices, blocks * pieces + EXTRA, BLOCK)
    row_block = pl.BlockSpec((each * BLOCK, width), lambda b, *_: (b, 0))
    return pl.pallas_call(
        lambda *refs: own_kernel(heads, blocks, each, *refs),
        grid_spec=pltpu.PrefetchScalarGridSpec(
            num_scalar_prefetch=2,
            grid=(blocks // each,),
            in_specs=[
                pl.BlockSpec(lengths.shape, lambda b, *_: (0, 0)),
                row_block,
                row_block,
                pl.BlockSpec((heads, each * BLOCK), lambda b, *_: (0, b)),
            ],
            out_specs=pl.BlockSpec(memory_space=pl.ANY),
            scratch_shapes=[
                pltpu.VMEM(shape, BF16),
                pltpu.VMEM((heads, blocks, BLOCK), F32),
                pltpu.VMEM((each, heads, BLOCK, BLOCK), BF16),
                pltpu.SemaphoreType.DMA((blocks // each + 1,)),
            ],
        ),
        out_shape=jax.ShapeDtypeStruct(shape, BF16),
        name="own",
    )(packing, place, lengths, keys, values, decay)


def intra_kernel(heads, packing, place, lengths, queries, keys, values, decay, intra, faded):
    block = pl.program_id(0)
    base = (packing[place[0] * pl.num_programs(0) + block] * BLOCK).astype(F32)
    along = dot(decay[...], triangle(True), (1, 0))
    down = dot(triangle(False), decay[...], (1, 1))
    row = lax.broadcasted_iota(jnp.int32, (BLOCK, BLOCK), 0)
    column = lax.broadcasted_iota(jnp.int32, (BLOCK, BLOCK), 1)
    begun = jnp.broadcast_to(start_row(lengths[...]), (BLOCK, BLOCK))
    begun = jnp.where(begun <= row.astype(F32) + base, begun, -FAR)
    started = jnp.max(begun, axis=1, keepdims=True)
    allowed = (column <= row) & (column.astype(F32) + base >= started)
    reach = jnp.exp(down) * jnp.where(started < base, 1.0, 0.0)
    for head in range(heads):
        span = slice(head * BLOCK, (head + 1) * BLOCK)
        query = queries[:, span]
        scores = dot(query, keys[:, span], (1, 1))
        gaps = jnp.minimum(down[:, head : head + 1] - along[head : head + 1, :], 0.0)
        weights = (scores * jnp.where(allowed, jnp.exp(gaps), 0.0)).astype(BF16)
        intra[:, span] = dot(weights, values[:, span], (1, 0))
        faded[:, span] = (query.astype(F32) * reach[:, head : head + 1]).astype(BF16)


def intra_pass(packing, place, lengths, queries, keys, values, decay):
    rows, width = queries.shape
    heads = decay.shape[0]
    row_block = pl.BlockSpec((BLOCK, width), lambda b, *_: (b, 0))
    return pl.pallas_call(
        lambda *refs: intra_kernel(heads, *refs),
        grid_spec=pltpu.PrefetchScalarGridSpec(
            num_scalar_prefetch=2,
            grid=(rows // BLOCK,),
            in_specs=[
                pl.BlockSpec(lengths.shape, lambda b, *_: (0, 0)),
                row_block,
                row_block,
                row_block,
                pl.BlockSpec((heads, BLOCK), lambda b, *_: (0, b)),
            ],
            out_specs=[row_block, row_block],
        ),
        out_shape=[
            jax.ShapeDtypeStruct((rows, width), F32),
            jax.ShapeDtypeStruct((rows, width), BF16),
        ],
        name="intra",
    )(packing, place, lengths, queries, keys, values, decay)


def scan_kernel(devices, blocks, order, own, prior, gates):
    each = own.shape[0] // devices
    parts = (each - 1) // blocks
    for device in range(devices):
        tile = own[(device + 1) * each - 1].astype(F32)
        gate = tile[:, 0:1] + tile[:, 1:2] + tile[:, 2:3]
        gates[device * blocks : (device + 1) * blocks, :] = jnp.broadcast_to(gate[:blocks], (blocks, BLOCK))

    def step(j, state):
        at = order[j]
        ahead = at * parts
        source = ahead + lax.shift_right_logical(at, blocks.bit_length() - 1)
        gate = gates[pl.ds(at, 1), :]
        after = []
        for part in range(parts):
            prior[ahead + part] = state[part].astype(BF16)
            after.append(gate * state[part] + own[source + part].astype(F32))
        return tuple(after)

    zero = jnp.zeros(own.shape[1:], F32)
    lax.fori_loop(0, devices * blocks, step, (zero,) * parts, unroll=16)


def scan_pass(order, own):
    devices, height, lanes = own.shape
    blocks = order.shape[0] // devices
    tiles = own.reshape(devices * height // EXTRA, EXTRA, lanes)
    vmem = pl.BlockSpec(memory_space=pltpu.VMEM)
    prior = pl.pallas_call(
        lambda *refs: scan_kernel(devices, blocks, *refs),
        in_specs=[pl.BlockSpec(memory_space=pltpu.SMEM), vmem],
        out_specs=vmem,
        out_shape=jax.ShapeDtypeStruct((tiles.shape[0] - devices, EXTRA, lanes), BF16),
        scratch_shapes=[pltpu.VMEM((devices * blocks, BLOCK), F32)],
        compiler_params=pltpu.CompilerParams(vmem_limit_bytes=20 * 2**20),
        name="scan",
    )(order, tiles)
    return prior.reshape(devices, height - EXTRA, lanes)


def outgo_kernel(heads, blocks, each, packing, place, faded, intra, states, slots, made, sems):
    step = pl.program_id(0)
    per_head = states.shape[0] // heads
    pieces = BLOCK // per_head
    row = lax.broadcasted_iota(jnp.int32, (TAIL, BLOCK), 0)

    def copy(block):
        owner = packing[place[0] * blocks + block] // blocks
        return pltpu.make_async_copy(made.at[block], slots.at[owner], sems.at[block])

    for inside in range(each):
        block = step * each + inside
        rows = slice(inside * BLOCK, (inside + 1) * BLOCK)
        sums = jnp.zeros((BLOCK, BLOCK), F32)
        for head in range(heads):
            span = slice(head * BLOCK, (head + 1) * BLOCK)
            state = states[
                head * per_head : (head + 1) * per_head, inside * pieces : (inside + 1) * pieces
            ].reshape(BLOCK, BLOCK)
            out = intra[rows, span] + dot(faded[rows, span], state, (1, 0))
            sums = sums + out * out
            made[block, span, :] = out.astype(BF16)
        high, middle, low = in_three(jnp.sum(sums.T, axis=0, keepdims=True))
        tile = jnp.where(row == 0, high, jnp.where(row == 1, middle, low))
        made[block, heads * BLOCK :, :] = tile.astype(BF16)
    for inside in range(each):
        copy(step * each + inside).start()

    @pl.when(step == pl.num_programs(0) - 1)
    def _():
        for block in range(blocks):
            copy(block).wait()


def outgo_pass(packing, place, faded, intra, states):
    rows, width = faded.shape
    blocks = rows // BLOCK
    devices, height, lanes = states.shape
    each = OUTGO_EACH
    heads = width // BLOCK
    row_block = pl.BlockSpec((each * BLOCK, width), lambda b, *_: (b, 0))
    return pl.pallas_call(
        lambda *refs: outgo_kernel(heads, blocks, each, *refs),
        grid_spec=pltpu.PrefetchScalarGridSpec(
            num_scalar_prefetch=2,
            grid=(blocks // each,),
            in_specs=[
                row_block,
                row_block,
                pl.BlockSpec((devices, height // blocks * each, lanes), lambda b, *_: (0, b, 0)),
            ],
            out_specs=pl.BlockSpec(memory_space=pl.ANY),
            scratch_shapes=[
                pltpu.VMEM((blocks, width + TAIL, BLOCK), BF16),
                pltpu.SemaphoreType.DMA((blocks,)),
            ],
        ),
        out_shape=jax.ShapeDtypeStruct((devices, width + TAIL, BLOCK), BF16),
        compiler_params=pltpu.CompilerParams(vmem_limit_bytes=18 * 2**20),
        name="outgo",
    )(packing, place, faded, intra, states)


def squares_kernel(order, place, came, squares, tiles, sems):
    blocks, extra, _ = tiles.shape
    height = came.shape[1] - extra

    def copy(block):
        loader = order[place[0] * blocks + block] // blocks
        return pltpu.make_async_copy(came.at[loader, height:], tiles.at[block], sems.at[block])

    for block in range(blocks):
        copy(block).start()
    for block in range(blocks):
        copy(block).wait()
        tile = tiles[block].astype(F32)
        squares[block : block + 1, :] = tile[0:1, :] + tile[1:2, :] + tile[2:3, :]


def squares_pass(order, place, came):
    blocks = order.shape[0] // came.shape[0]
    smem = pl.BlockSpec(memory_space=pltpu.SMEM)
    return pl.pallas_call(
        squares_kernel,
        in_specs=[smem, smem, pl.BlockSpec(memory_space=pl.ANY)],
        out_specs=pl.BlockSpec(memory_space=pltpu.VMEM),
        out_shape=jax.ShapeDtypeStruct((blocks, BLOCK), F32),
        scratch_shapes=[
            pltpu.VMEM((blocks, TAIL, BLOCK), BF16),
            pltpu.SemaphoreType.DMA((blocks,)),
        ],
        compiler_params=pltpu.CompilerParams(vmem_limit_bytes=2 * 2**20),
        name="squares",
    )(order, place, came)


def finish_kernel(groups, each, order, place, *refs):
    squares, gain, parts, mixed = refs[:groups], refs[groups], refs[groups + 1 : -1], refs[-1]
    width = gain.shape[1]
    for inside in range(each):
        block = pl.ds(pl.program_id(0) * each + inside, 1)
        total = squares[0][block, :]
        for other in squares[1:]:
            total = total + other[block, :]
        scale = lax.rsqrt(total / (width * groups) + 1e-05)
        scale = jnp.broadcast_to(scale, (BLOCK, BLOCK)).T
        rows = slice(inside * BLOCK, (inside + 1) * BLOCK)
        for head in range(width // BLOCK):
            span = slice(head * BLOCK, (head + 1) * BLOCK)
            out = parts[inside][0, span, :].astype(F32) * scale * gain[:, span]
            mixed[rows, span] = out.astype(BF16)


def finish_pass(order, place, squares, gain, came):
    devices, height, lanes = came.shape
    blocks = order.shape[0] // devices
    width = gain.shape[1]
    each = FINISH_EACH

    def part(inside):
        def loader(b, order, place):
            return order[place[0] * blocks + b * each + inside] // blocks, 0, 0

        return pl.BlockSpec((1, width, lanes), loader)

    return pl.pallas_call(
        lambda *refs: finish_kernel(len(squares), each, *refs),
        grid_spec=pltpu.PrefetchScalarGridSpec(
            num_scalar_prefetch=2,
            grid=(blocks // each,),
            in_specs=[pl.BlockSpec((blocks, BLOCK), lambda b, *_: (0, 0))] * len(squares)
            + [pl.BlockSpec((1, width), lambda b, *_: (0, 0))]
            + [part(inside) for inside in range(each)],
            out_specs=pl.BlockSpec((each * BLOCK, width), lambda b, *_: (b, 0)),
        ),
        out_shape=jax.ShapeDtypeStruct((blocks * BLOCK, width), BF16),
        compiler_params=pltpu.CompilerParams(vmem_limit_bytes=14 * 2**20),
        name="finish",
    )(order, place, *squares, gain, *[came] * each)


def swap(x, axis):
    return lax.all_to_all(x, axis, split_axis=0, concat_axis=0, tiled=True)


def body(queries, key_rows, value_rows, log_decay, norm_gain, doc_lengths, packing):
    mine = lax.axis_index("ctx").astype(jnp.int32)
    place = mine.reshape(1)
    decay = log_decay.T
    lengths = doc_lengths[None, :]

    index = jnp.arange(packing.shape[0], dtype=jnp.int32)
    hit = (packing[None, :] == index[:, None]).astype(jnp.int32)
    order = jnp.sum(hit * index[None, :], axis=1)

    own = swap(own_states(packing, place, lengths, key_rows, value_rows, decay), "ctx")
    intra, faded = intra_pass(packing, place, lengths, queries, key_rows, value_rows, decay)

    own, order, intra, faded = lax.optimization_barrier((own, order, intra, faded))
    prior = scan_pass(order, own)
    prior, intra, faded = lax.optimization_barrier((prior, intra, faded))
    states = swap(prior, "ctx")
    came = swap(outgo_pass(packing, place, faded, intra, states), "ctx")
    part = squares_pass(order, place, came)
    groups = lax.axis_size("head")
    squares = [part]
    for shift in range(1, groups):
        pairs = [(i, (i + shift) % groups) for i in range(groups)]
        squares.append(lax.ppermute(part, "head", pairs))
    return finish_pass(order, place, squares, norm_gain[None, :], came)


def solution(mesh):
    placed = (
        P("ctx", "head"),
        P("ctx", "head"),
        P("ctx", "head"),
        P("ctx", "head"),
        P("head"),
        P(),
        P(),
    )
    return jax.shard_map(
        body, mesh=mesh, in_specs=placed, out_specs=P("ctx", "head"), check_vma=False
    )
```

```python
import jax
import jax.numpy as jnp
from jax import lax
from jax.experimental import pallas as pl
from jax.experimental.pallas import tpu as pltpu
from jax.sharding import PartitionSpec as P

BLOCK = 128
EXTRA = 16
TAIL = 8
FAR = 1e9
OWN_EACH = 8
OUTGO_EACH = 8
FINISH_EACH = 8
F32 = jnp.float32
BF16 = jnp.bfloat16


def dot(a, b, contract):
    return lax.dot_general(a, b, ((contract[:1], contract[1:]), ((), ())), preferred_element_type=F32)


def triangle(upper):
    row = lax.broadcasted_iota(jnp.int32, (BLOCK, BLOCK), 0)
    column = lax.broadcasted_iota(jnp.int32, (BLOCK, BLOCK), 1)
    keep = row <= column if upper else column <= row
    return jnp.where(keep, 1.0, 0.0).astype(BF16)


def in_three(x):
    high = x.astype(BF16).astype(F32)
    middle = (x - high).astype(BF16).astype(F32)
    return high, middle, x - high - middle


def start_row(lengths):
    count = lengths.shape[1]
    row = lax.broadcasted_iota(jnp.int32, (count, BLOCK), 0)
    ahead = jnp.where(row < lax.broadcasted_iota(jnp.int32, (count, BLOCK), 1), 1.0, 0.0)
    wide = jnp.broadcast_to(lengths.astype(F32), (8, count))
    return lax.dot_general(
        wide, ahead, (((1,), (0,)), ((), ())), precision=lax.Precision.HIGHEST, preferred_element_type=F32
    )[:1]


def own_kernel(heads, blocks, each, packing, place, lengths, keys, values, decay, own, made, fates, faded, sems):
    step = pl.program_id(0)
    per_head = made.shape[0] // heads
    pieces = BLOCK // per_head
    steps = blocks // each
    upper = triangle(True)
    starts = start_row(lengths[...])
    lane = lax.broadcasted_iota(jnp.int32, (1, BLOCK), 1).astype(F32)
    keeps = []
    for inside in range(each):
        block = step * each + inside
        rows = slice(inside * BLOCK, (inside + 1) * BLOCK)
        base = (packing[place[0] * blocks + block] * BLOCK).astype(F32)
        logs = dot(decay[:, rows], upper, (1, 0))
        total = logs[:, BLOCK - 1 :]
        begun = jnp.where(starts <= base + (BLOCK - 1), starts, -FAR)
        started = jnp.max(begun, axis=1, keepdims=True)
        keeps.append(jnp.exp(total - logs) * jnp.where(lane + base >= started, 1.0, 0.0))
        gate = jnp.exp(total) * jnp.where(started < base, 1.0, 0.0)
        for head in range(heads):
            fates[head, pl.ds(block, 1), :] = jnp.broadcast_to(gate[head : head + 1, :], (1, BLOCK))

    def fade(inside, head):
        rows = slice(inside * BLOCK, (inside + 1) * BLOCK)
        span = slice(head * BLOCK, (head + 1) * BLOCK)
        turned = keys[rows, span].T.astype(F32) * keeps[inside][head : head + 1, :]
        faded[inside, head] = turned.astype(BF16)

    def multiply(inside, head):
        rows = slice(inside * BLOCK, (inside + 1) * BLOCK)
        span = slice(head * BLOCK, (head + 1) * BLOCK)
        state = dot(faded[inside, head], values[rows, span], (1, 0)).astype(BF16)
        to = pl.ds(pl.multiple_of((step * each + inside) * pieces, pieces), pieces)
        made[head * per_head : (head + 1) * per_head, to] = state.reshape(per_head, pieces, BLOCK)

    for inside in range(each + 1):
        for head in range(heads):
            if inside < each:
                fade(inside, head)
            if inside:
                multiply(inside - 1, head)

    def copy(at, start, size):
        part = (slice(None), pl.ds(start, size))
        return pltpu.make_async_copy(made.at[part], own.at[part], sems.at[at])

    span = each * pieces
    copy(step, pl.multiple_of(step * span, span), span).start()

    @pl.when(step == steps - 1)
    def _():
        at = lax.broadcasted_iota(jnp.int32, (EXTRA, BLOCK), 1)
        for head in range(heads):
            high, middle, low = in_three(fates[head])
            tile = jnp.where(at == 0, high, jnp.where(at == 1, middle, low)).astype(BF16)
            for piece in range(per_head):
                made[head * per_head + piece, blocks * pieces :] = tile
        copy(steps, blocks * pieces, EXTRA).start()
        for earlier in range(steps):
            copy(earlier, earlier * span, span).wait()
        copy(steps, blocks * pieces, EXTRA).wait()


def own_states(packing, place, lengths, keys, values, decay):
    rows, width = keys.shape
    heads = decay.shape[0]
    blocks = rows // BLOCK
    each = OWN_EACH
    devices = packing.shape[0] // blocks
    pieces = heads * BLOCK // devices
    shape = (devices, blocks * pieces + EXTRA, BLOCK)
    row_block = pl.BlockSpec((each * BLOCK, width), lambda b, *_: (b, 0))
    return pl.pallas_call(
        lambda *refs: own_kernel(heads, blocks, each, *refs),
        grid_spec=pltpu.PrefetchScalarGridSpec(
            num_scalar_prefetch=2,
            grid=(blocks // each,),
            in_specs=[
                pl.BlockSpec(lengths.shape, lambda b, *_: (0, 0)),
                row_block,
                row_block,
                pl.BlockSpec((heads, each * BLOCK), lambda b, *_: (0, b)),
            ],
            out_specs=pl.BlockSpec(memory_space=pl.ANY),
            scratch_shapes=[
                pltpu.VMEM(shape, BF16),
                pltpu.VMEM((heads, blocks, BLOCK), F32),
                pltpu.VMEM((each, heads, BLOCK, BLOCK), BF16),
                pltpu.SemaphoreType.DMA((blocks // each + 1,)),
            ],
        ),
        out_shape=jax.ShapeDtypeStruct(shape, BF16),
        name="own",
    )(packing, place, lengths, keys, values, decay)


def intra_kernel(heads, packing, place, lengths, queries, keys, values, decay, intra, faded):
    block = pl.program_id(0)
    base = (packing[place[0] * pl.num_programs(0) + block] * BLOCK).astype(F32)
    along = dot(decay[...], triangle(True), (1, 0))
    down = dot(triangle(False), decay[...], (1, 1))
    row = lax.broadcasted_iota(jnp.int32, (BLOCK, BLOCK), 0)
    column = lax.broadcasted_iota(jnp.int32, (BLOCK, BLOCK), 1)
    begun = jnp.broadcast_to(start_row(lengths[...]), (BLOCK, BLOCK))
    begun = jnp.where(begun <= row.astype(F32) + base, begun, -FAR)
    started = jnp.max(begun, axis=1, keepdims=True)
    allowed = (column <= row) & (column.astype(F32) + base >= started)
    reach = jnp.exp(down) * jnp.where(started < base, 1.0, 0.0)
    for head in range(heads):
        span = slice(head * BLOCK, (head + 1) * BLOCK)
        query = queries[:, span]
        scores = dot(query, keys[:, span], (1, 1))
        gaps = jnp.minimum(down[:, head : head + 1] - along[head : head + 1, :], 0.0)
        weights = (scores * jnp.where(allowed, jnp.exp(gaps), 0.0)).astype(BF16)
        intra[:, span] = dot(weights, values[:, span], (1, 0))
        faded[:, span] = (query.astype(F32) * reach[:, head : head + 1]).astype(BF16)


def intra_pass(packing, place, lengths, queries, keys, values, decay):
    rows, width = queries.shape
    heads = decay.shape[0]
    row_block = pl.BlockSpec((BLOCK, width), lambda b, *_: (b, 0))
    return pl.pallas_call(
        lambda *refs: intra_kernel(heads, *refs),
        grid_spec=pltpu.PrefetchScalarGridSpec(
            num_scalar_prefetch=2,
            grid=(rows // BLOCK,),
            in_specs=[
                pl.BlockSpec(lengths.shape, lambda b, *_: (0, 0)),
                row_block,
                row_block,
                row_block,
                pl.BlockSpec((heads, BLOCK), lambda b, *_: (0, b)),
            ],
            out_specs=[row_block, row_block],
        ),
        out_shape=[
            jax.ShapeDtypeStruct((rows, width), F32),
            jax.ShapeDtypeStruct((rows, width), BF16),
        ],
        name="intra",
    )(packing, place, lengths, queries, keys, values, decay)


def scan_kernel(devices, blocks, order, own, prior, gates):
    each = own.shape[0] // devices
    parts = (each - 1) // blocks
    for device in range(devices):
        tile = own[(device + 1) * each - 1].astype(F32)
        gate = tile[:, 0:1] + tile[:, 1:2] + tile[:, 2:3]
        gates[device * blocks : (device + 1) * blocks, :] = jnp.broadcast_to(gate[:blocks], (blocks, BLOCK))

    def step(j, state):
        at = order[j]
        ahead = at * parts
        source = ahead + lax.shift_right_logical(at, blocks.bit_length() - 1)
        gate = gates[pl.ds(at, 1), :]
        after = []
        for part in range(parts):
            prior[ahead + part] = state[part].astype(BF16)
            after.append(gate * state[part] + own[source + part].astype(F32))
        return tuple(after)

    zero = jnp.zeros(own.shape[1:], F32)
    lax.fori_loop(0, devices * blocks, step, (zero,) * parts, unroll=16)


def scan_pass(order, own):
    devices, height, lanes = own.shape
    blocks = order.shape[0] // devices
    tiles = own.reshape(devices * height // EXTRA, EXTRA, lanes)
    vmem = pl.BlockSpec(memory_space=pltpu.VMEM)
    prior = pl.pallas_call(
        lambda *refs: scan_kernel(devices, blocks, *refs),
        in_specs=[pl.BlockSpec(memory_space=pltpu.SMEM), vmem],
        out_specs=vmem,
        out_shape=jax.ShapeDtypeStruct((tiles.shape[0] - devices, EXTRA, lanes), BF16),
        scratch_shapes=[pltpu.VMEM((devices * blocks, BLOCK), F32)],
        compiler_params=pltpu.CompilerParams(vmem_limit_bytes=20 * 2**20),
        name="scan",
    )(order, tiles)
    return prior.reshape(devices, height - EXTRA, lanes)


def outgo_kernel(heads, blocks, each, packing, place, faded, intra, states, slots, made, sems):
    step = pl.program_id(0)
    per_head = states.shape[0] // heads
    pieces = BLOCK // per_head
    row = lax.broadcasted_iota(jnp.int32, (TAIL, BLOCK), 0)

    def copy(block):
        owner = packing[place[0] * blocks + block] // blocks
        return pltpu.make_async_copy(made.at[block], slots.at[owner], sems.at[block])

    for inside in range(each):
        block = step * each + inside
        rows = slice(inside * BLOCK, (inside + 1) * BLOCK)
        sums = jnp.zeros((BLOCK, BLOCK), F32)
        for head in range(heads):
            span = slice(head * BLOCK, (head + 1) * BLOCK)
            state = states[
                head * per_head : (head + 1) * per_head, inside * pieces : (inside + 1) * pieces
            ].reshape(BLOCK, BLOCK)
            out = intra[rows, span] + dot(faded[rows, span], state, (1, 0))
            sums = sums + out * out
            made[block, span, :] = out.astype(BF16)
        high, middle, low = in_three(jnp.sum(sums.T, axis=0, keepdims=True))
        tile = jnp.where(row == 0, high, jnp.where(row == 1, middle, low))
        made[block, heads * BLOCK :, :] = tile.astype(BF16)
    for inside in range(each):
        copy(step * each + inside).start()

    @pl.when(step == pl.num_programs(0) - 1)
    def _():
        for block in range(blocks):
            copy(block).wait()


def outgo_pass(packing, place, faded, intra, states):
    rows, width = faded.shape
    blocks = rows // BLOCK
    devices, height, lanes = states.shape
    each = OUTGO_EACH
    heads = width // BLOCK
    row_block = pl.BlockSpec((each * BLOCK, width), lambda b, *_: (b, 0))
    return pl.pallas_call(
        lambda *refs: outgo_kernel(heads, blocks, each, *refs),
        grid_spec=pltpu.PrefetchScalarGridSpec(
            num_scalar_prefetch=2,
            grid=(blocks // each,),
            in_specs=[
                row_block,
                row_block,
                pl.BlockSpec((devices, height // blocks * each, lanes), lambda b, *_: (0, b, 0)),
            ],
            out_specs=pl.BlockSpec(memory_space=pl.ANY),
            scratch_shapes=[
                pltpu.VMEM((blocks, width + TAIL, BLOCK), BF16),
                pltpu.SemaphoreType.DMA((blocks,)),
            ],
        ),
        out_shape=jax.ShapeDtypeStruct((devices, width + TAIL, BLOCK), BF16),
        compiler_params=pltpu.CompilerParams(vmem_limit_bytes=24 * 2**20),
        name="outgo",
    )(packing, place, faded, intra, states)


def squares_kernel(order, place, came, squares, tiles, sems):
    blocks, extra, _ = tiles.shape
    height = came.shape[1] - extra

    def copy(block):
        loader = order[place[0] * blocks + block] // blocks
        return pltpu.make_async_copy(came.at[loader, height:], tiles.at[block], sems.at[block])

    for block in range(blocks):
        copy(block).start()
    for block in range(blocks):
        copy(block).wait()
        tile = tiles[block].astype(F32)
        squares[block : block + 1, :] = tile[0:1, :] + tile[1:2, :] + tile[2:3, :]


def squares_pass(order, place, came):
    blocks = order.shape[0] // came.shape[0]
    smem = pl.BlockSpec(memory_space=pltpu.SMEM)
    return pl.pallas_call(
        squares_kernel,
        in_specs=[smem, smem, pl.BlockSpec(memory_space=pl.ANY)],
        out_specs=pl.BlockSpec(memory_space=pltpu.VMEM),
        out_shape=jax.ShapeDtypeStruct((blocks, BLOCK), F32),
        scratch_shapes=[
            pltpu.VMEM((blocks, TAIL, BLOCK), BF16),
            pltpu.SemaphoreType.DMA((blocks,)),
        ],
        compiler_params=pltpu.CompilerParams(vmem_limit_bytes=2 * 2**20),
        name="squares",
    )(order, place, came)


def finish_kernel(groups, each, order, place, *refs):
    squares, gain, parts, mixed = refs[:groups], refs[groups], refs[groups + 1 : -1], refs[-1]
    width = gain.shape[1]
    for inside in range(each):
        block = pl.ds(pl.program_id(0) * each + inside, 1)
        total = squares[0][block, :]
        for other in squares[1:]:
            total = total + other[block, :]
        scale = lax.rsqrt(total / (width * groups) + 1e-05)
        scale = jnp.broadcast_to(scale, (BLOCK, BLOCK)).T
        rows = slice(inside * BLOCK, (inside + 1) * BLOCK)
        for head in range(width // BLOCK):
            span = slice(head * BLOCK, (head + 1) * BLOCK)
            out = parts[inside][0, span, :].astype(F32) * scale * gain[:, span]
            mixed[rows, span] = out.astype(BF16)


def finish_pass(order, place, squares, gain, came):
    devices, height, lanes = came.shape
    blocks = order.shape[0] // devices
    width = gain.shape[1]
    each = FINISH_EACH

    def part(inside):
        def loader(b, order, place):
            return order[place[0] * blocks + b * each + inside] // blocks, 0, 0

        return pl.BlockSpec((1, width, lanes), loader)

    return pl.pallas_call(
        lambda *refs: finish_kernel(len(squares), each, *refs),
        grid_spec=pltpu.PrefetchScalarGridSpec(
            num_scalar_prefetch=2,
            grid=(blocks // each,),
            in_specs=[pl.BlockSpec((blocks, BLOCK), lambda b, *_: (0, 0))] * len(squares)
            + [pl.BlockSpec((1, width), lambda b, *_: (0, 0))]
            + [part(inside) for inside in range(each)],
            out_specs=pl.BlockSpec((each * BLOCK, width), lambda b, *_: (b, 0)),
        ),
        out_shape=jax.ShapeDtypeStruct((blocks * BLOCK, width), BF16),
        compiler_params=pltpu.CompilerParams(vmem_limit_bytes=14 * 2**20),
        name="finish",
    )(order, place, *squares, gain, *[came] * each)


def swap(x, axis):
    return lax.all_to_all(x, axis, split_axis=0, concat_axis=0, tiled=True)


def body(queries, key_rows, value_rows, log_decay, norm_gain, doc_lengths, packing):
    mine = lax.axis_index("ctx").astype(jnp.int32)
    place = mine.reshape(1)
    decay = log_decay.T
    lengths = doc_lengths[None, :]

    index = jnp.arange(packing.shape[0], dtype=jnp.int32)
    hit = (packing[None, :] == index[:, None]).astype(jnp.int32)
    order = jnp.sum(hit * index[None, :], axis=1)

    own = swap(own_states(packing, place, lengths, key_rows, value_rows, decay), "ctx")
    intra, faded = intra_pass(packing, place, lengths, queries, key_rows, value_rows, decay)

    own, order, intra, faded = lax.optimization_barrier((own, order, intra, faded))
    prior = scan_pass(order, own)
    prior, intra, faded = lax.optimization_barrier((prior, intra, faded))
    states = swap(prior, "ctx")
    came = swap(outgo_pass(packing, place, faded, intra, states), "ctx")
    part = squares_pass(order, place, came)
    groups = lax.axis_size("head")
    squares = [part]
    for shift in range(1, groups):
        pairs = [(i, (i + shift) % groups) for i in range(groups)]
        squares.append(lax.ppermute(part, "head", pairs))
    return finish_pass(order, place, squares, norm_gain[None, :], came)


def solution(mesh):
    placed = (
        P("ctx", "head"),
        P("ctx", "head"),
        P("ctx", "head"),
        P("ctx", "head"),
        P("head"),
        P(),
        P(),
    )
    return jax.shard_map(
        body, mesh=mesh, in_specs=placed, out_specs=P("ctx", "head"), check_vma=False
    )
```

```python
import jax
import jax.numpy as jnp
from jax import lax
from jax.experimental import pallas as pl
from jax.experimental.pallas import tpu as pltpu
from jax.sharding import PartitionSpec as P

BLOCK = 128
EXTRA = 16
TAIL = 8
FAR = 1e9
OWN_EACH = 8
OUTGO_EACH = 4
FINISH_EACH = 8
F32 = jnp.float32
BF16 = jnp.bfloat16


def dot(a, b, contract):
    return lax.dot_general(a, b, ((contract[:1], contract[1:]), ((), ())), preferred_element_type=F32)


def triangle(upper):
    row = lax.broadcasted_iota(jnp.int32, (BLOCK, BLOCK), 0)
    column = lax.broadcasted_iota(jnp.int32, (BLOCK, BLOCK), 1)
    keep = row <= column if upper else column <= row
    return jnp.where(keep, 1.0, 0.0).astype(BF16)


def in_three(x):
    high = x.astype(BF16).astype(F32)
    middle = (x - high).astype(BF16).astype(F32)
    return high, middle, x - high - middle


def start_row(lengths):
    count = lengths.shape[1]
    row = lax.broadcasted_iota(jnp.int32, (count, BLOCK), 0)
    ahead = jnp.where(row < lax.broadcasted_iota(jnp.int32, (count, BLOCK), 1), 1.0, 0.0)
    wide = jnp.broadcast_to(lengths.astype(F32), (8, count))
    return lax.dot_general(
        wide, ahead, (((1,), (0,)), ((), ())), precision=lax.Precision.HIGHEST, preferred_element_type=F32
    )[:1]


def own_kernel(heads, blocks, each, packing, place, lengths, keys, values, decay, own, made, fates, faded, sems):
    step = pl.program_id(0)
    per_head = made.shape[0] // heads
    pieces = BLOCK // per_head
    steps = blocks // each
    upper = triangle(True)
    starts = start_row(lengths[...])
    lane = lax.broadcasted_iota(jnp.int32, (1, BLOCK), 1).astype(F32)
    keeps = []
    for inside in range(each):
        block = step * each + inside
        rows = slice(inside * BLOCK, (inside + 1) * BLOCK)
        base = (packing[place[0] * blocks + block] * BLOCK).astype(F32)
        logs = dot(decay[:, rows], upper, (1, 0))
        total = logs[:, BLOCK - 1 :]
        begun = jnp.where(starts <= base + (BLOCK - 1), starts, -FAR)
        started = jnp.max(begun, axis=1, keepdims=True)
        keeps.append(jnp.exp(total - logs) * jnp.where(lane + base >= started, 1.0, 0.0))
        gate = jnp.exp(total) * jnp.where(started < base, 1.0, 0.0)
        for head in range(heads):
            fates[head, pl.ds(block, 1), :] = jnp.broadcast_to(gate[head : head + 1, :], (1, BLOCK))

    def fade(inside, head):
        rows = slice(inside * BLOCK, (inside + 1) * BLOCK)
        span = slice(head * BLOCK, (head + 1) * BLOCK)
        turned = keys[rows, span].T.astype(F32) * keeps[inside][head : head + 1, :]
        faded[inside, head] = turned.astype(BF16)

    def multiply(inside, head):
        rows = slice(inside * BLOCK, (inside + 1) * BLOCK)
        span = slice(head * BLOCK, (head + 1) * BLOCK)
        state = dot(faded[inside, head], values[rows, span], (1, 0)).astype(BF16)
        to = pl.ds(pl.multiple_of((step * each + inside) * pieces, pieces), pieces)
        made[head * per_head : (head + 1) * per_head, to] = state.reshape(per_head, pieces, BLOCK)

    for inside in range(each + 1):
        for head in range(heads):
            if inside < each:
                fade(inside, head)
            if inside:
                multiply(inside - 1, head)

    def copy(at, start, size):
        part = (slice(None), pl.ds(start, size))
        return pltpu.make_async_copy(made.at[part], own.at[part], sems.at[at])

    span = each * pieces
    copy(step, pl.multiple_of(step * span, span), span).start()

    @pl.when(step == steps - 1)
    def _():
        at = lax.broadcasted_iota(jnp.int32, (EXTRA, BLOCK), 1)
        for head in range(heads):
            high, middle, low = in_three(fates[head])
            tile = jnp.where(at == 0, high, jnp.where(at == 1, middle, low)).astype(BF16)
            for piece in range(per_head):
                made[head * per_head + piece, blocks * pieces :] = tile
        copy(steps, blocks * pieces, EXTRA).start()
        for earlier in range(steps):
            copy(earlier, earlier * span, span).wait()
        copy(steps, blocks * pieces, EXTRA).wait()


def own_states(packing, place, lengths, keys, values, decay):
    rows, width = keys.shape
    heads = decay.shape[0]
    blocks = rows // BLOCK
    each = OWN_EACH
    devices = packing.shape[0] // blocks
    pieces = heads * BLOCK // devices
    shape = (devices, blocks * pieces + EXTRA, BLOCK)
    row_block = pl.BlockSpec((each * BLOCK, width), lambda b, *_: (b, 0))
    return pl.pallas_call(
        lambda *refs: own_kernel(heads, blocks, each, *refs),
        grid_spec=pltpu.PrefetchScalarGridSpec(
            num_scalar_prefetch=2,
            grid=(blocks // each,),
            in_specs=[
                pl.BlockSpec(lengths.shape, lambda b, *_: (0, 0)),
                row_block,
                row_block,
                pl.BlockSpec((heads, each * BLOCK), lambda b, *_: (0, b)),
            ],
            out_specs=pl.BlockSpec(memory_space=pl.ANY),
            scratch_shapes=[
                pltpu.VMEM(shape, BF16),
                pltpu.VMEM((heads, blocks, BLOCK), F32),
                pltpu.VMEM((each, heads, BLOCK, BLOCK), BF16),
                pltpu.SemaphoreType.DMA((blocks // each + 1,)),
            ],
        ),
        out_shape=jax.ShapeDtypeStruct(shape, BF16),
        name="own",
    )(packing, place, lengths, keys, values, decay)


def intra_kernel(heads, packing, place, lengths, queries, keys, values, decay, intra, faded):
    block = pl.program_id(0)
    base = (packing[place[0] * pl.num_programs(0) + block] * BLOCK).astype(F32)
    along = dot(decay[...], triangle(True), (1, 0))
    down = dot(triangle(False), decay[...], (1, 1))
    row = lax.broadcasted_iota(jnp.int32, (BLOCK, BLOCK), 0)
    column = lax.broadcasted_iota(jnp.int32, (BLOCK, BLOCK), 1)
    begun = jnp.broadcast_to(start_row(lengths[...]), (BLOCK, BLOCK))
    begun = jnp.where(begun <= row.astype(F32) + base, begun, -FAR)
    started = jnp.max(begun, axis=1, keepdims=True)
    allowed = (column <= row) & (column.astype(F32) + base >= started)
    reach = jnp.exp(down) * jnp.where(started < base, 1.0, 0.0)
    for head in range(heads):
        span = slice(head * BLOCK, (head + 1) * BLOCK)
        query = queries[:, span]
        scores = dot(query, keys[:, span], (1, 1))
        gaps = jnp.minimum(down[:, head : head + 1] - along[head : head + 1, :], 0.0)
        weights = (scores * jnp.where(allowed, jnp.exp(gaps), 0.0)).astype(BF16)
        intra[:, span] = dot(weights, values[:, span], (1, 0))
        faded[:, span] = (query.astype(F32) * reach[:, head : head + 1]).astype(BF16)


def intra_pass(packing, place, lengths, queries, keys, values, decay):
    rows, width = queries.shape
    heads = decay.shape[0]
    row_block = pl.BlockSpec((BLOCK, width), lambda b, *_: (b, 0))
    return pl.pallas_call(
        lambda *refs: intra_kernel(heads, *refs),
        grid_spec=pltpu.PrefetchScalarGridSpec(
            num_scalar_prefetch=2,
            grid=(rows // BLOCK,),
            in_specs=[
                pl.BlockSpec(lengths.shape, lambda b, *_: (0, 0)),
                row_block,
                row_block,
                row_block,
                pl.BlockSpec((heads, BLOCK), lambda b, *_: (0, b)),
            ],
            out_specs=[row_block, row_block],
        ),
        out_shape=[
            jax.ShapeDtypeStruct((rows, width), F32),
            jax.ShapeDtypeStruct((rows, width), BF16),
        ],
        name="intra",
    )(packing, place, lengths, queries, keys, values, decay)


def scan_kernel(devices, blocks, order, own, prior, gates):
    each = own.shape[0] // devices
    parts = (each - 1) // blocks
    for device in range(devices):
        tile = own[(device + 1) * each - 1].astype(F32)
        gate = tile[:, 0:1] + tile[:, 1:2] + tile[:, 2:3]
        gates[device * blocks : (device + 1) * blocks, :] = jnp.broadcast_to(gate[:blocks], (blocks, BLOCK))

    def step(j, state):
        at = order[j]
        ahead = at * parts
        source = ahead + lax.shift_right_logical(at, blocks.bit_length() - 1)
        gate = gates[pl.ds(at, 1), :]
        after = []
        for part in range(parts):
            prior[ahead + part] = state[part].astype(BF16)
            after.append(gate * state[part] + own[source + part].astype(F32))
        return tuple(after)

    zero = jnp.zeros(own.shape[1:], F32)
    lax.fori_loop(0, devices * blocks, step, (zero,) * parts, unroll=32)


def scan_pass(order, own):
    devices, height, lanes = own.shape
    blocks = order.shape[0] // devices
    tiles = own.reshape(devices * height // EXTRA, EXTRA, lanes)
    vmem = pl.BlockSpec(memory_space=pltpu.VMEM)
    prior = pl.pallas_call(
        lambda *refs: scan_kernel(devices, blocks, *refs),
        in_specs=[pl.BlockSpec(memory_space=pltpu.SMEM), vmem],
        out_specs=vmem,
        out_shape=jax.ShapeDtypeStruct((tiles.shape[0] - devices, EXTRA, lanes), BF16),
        scratch_shapes=[pltpu.VMEM((devices * blocks, BLOCK), F32)],
        compiler_params=pltpu.CompilerParams(vmem_limit_bytes=20 * 2**20),
        name="scan",
    )(order, tiles)
    return prior.reshape(devices, height - EXTRA, lanes)


def outgo_kernel(heads, blocks, each, packing, place, faded, intra, states, slots, made, sems):
    step = pl.program_id(0)
    per_head = states.shape[0] // heads
    pieces = BLOCK // per_head
    row = lax.broadcasted_iota(jnp.int32, (TAIL, BLOCK), 0)

    def copy(block):
        owner = packing[place[0] * blocks + block] // blocks
        return pltpu.make_async_copy(made.at[block], slots.at[owner], sems.at[block])

    for inside in range(each):
        block = step * each + inside
        rows = slice(inside * BLOCK, (inside + 1) * BLOCK)
        sums = jnp.zeros((BLOCK, BLOCK), F32)
        for head in range(heads):
            span = slice(head * BLOCK, (head + 1) * BLOCK)
            state = states[
                head * per_head : (head + 1) * per_head, inside * pieces : (inside + 1) * pieces
            ].reshape(BLOCK, BLOCK)
            out = intra[rows, span] + dot(faded[rows, span], state, (1, 0))
            sums = sums + out * out
            made[block, span, :] = out.astype(BF16)
        high, middle, low = in_three(jnp.sum(sums.T, axis=0, keepdims=True))
        tile = jnp.where(row == 0, high, jnp.where(row == 1, middle, low))
        made[block, heads * BLOCK :, :] = tile.astype(BF16)
    for inside in range(each):
        copy(step * each + inside).start()

    @pl.when(step == pl.num_programs(0) - 1)
    def _():
        for block in range(blocks):
            copy(block).wait()


def outgo_pass(packing, place, faded, intra, states):
    rows, width = faded.shape
    blocks = rows // BLOCK
    devices, height, lanes = states.shape
    each = OUTGO_EACH
    heads = width // BLOCK
    row_block = pl.BlockSpec((each * BLOCK, width), lambda b, *_: (b, 0))
    return pl.pallas_call(
        lambda *refs: outgo_kernel(heads, blocks, each, *refs),
        grid_spec=pltpu.PrefetchScalarGridSpec(
            num_scalar_prefetch=2,
            grid=(blocks // each,),
            in_specs=[
                row_block,
                row_block,
                pl.BlockSpec((devices, height // blocks * each, lanes), lambda b, *_: (0, b, 0)),
            ],
            out_specs=pl.BlockSpec(memory_space=pl.ANY),
            scratch_shapes=[
                pltpu.VMEM((blocks, width + TAIL, BLOCK), BF16),
                pltpu.SemaphoreType.DMA((blocks,)),
            ],
        ),
        out_shape=jax.ShapeDtypeStruct((devices, width + TAIL, BLOCK), BF16),
        compiler_params=pltpu.CompilerParams(vmem_limit_bytes=18 * 2**20),
        name="outgo",
    )(packing, place, faded, intra, states)


def squares_kernel(order, place, came, squares, tiles, sems):
    blocks, extra, _ = tiles.shape
    height = came.shape[1] - extra

    def copy(block):
        loader = order[place[0] * blocks + block] // blocks
        return pltpu.make_async_copy(came.at[loader, height:], tiles.at[block], sems.at[block])

    for block in range(blocks):
        copy(block).start()
    for block in range(blocks):
        copy(block).wait()
        tile = tiles[block].astype(F32)
        squares[block : block + 1, :] = tile[0:1, :] + tile[1:2, :] + tile[2:3, :]


def squares_pass(order, place, came):
    blocks = order.shape[0] // came.shape[0]
    smem = pl.BlockSpec(memory_space=pltpu.SMEM)
    return pl.pallas_call(
        squares_kernel,
        in_specs=[smem, smem, pl.BlockSpec(memory_space=pl.ANY)],
        out_specs=pl.BlockSpec(memory_space=pltpu.VMEM),
        out_shape=jax.ShapeDtypeStruct((blocks, BLOCK), F32),
        scratch_shapes=[
            pltpu.VMEM((blocks, TAIL, BLOCK), BF16),
            pltpu.SemaphoreType.DMA((blocks,)),
        ],
        compiler_params=pltpu.CompilerParams(vmem_limit_bytes=2 * 2**20),
        name="squares",
    )(order, place, came)


def finish_kernel(groups, each, order, place, *refs):
    squares, gain, parts, mixed = refs[:groups], refs[groups], refs[groups + 1 : -1], refs[-1]
    width = gain.shape[1]
    for inside in range(each):
        block = pl.ds(pl.program_id(0) * each + inside, 1)
        total = squares[0][block, :]
        for other in squares[1:]:
            total = total + other[block, :]
        scale = lax.rsqrt(total / (width * groups) + 1e-05)
        scale = jnp.broadcast_to(scale, (BLOCK, BLOCK)).T
        rows = slice(inside * BLOCK, (inside + 1) * BLOCK)
        for head in range(width // BLOCK):
            span = slice(head * BLOCK, (head + 1) * BLOCK)
            out = parts[inside][0, span, :].astype(F32) * scale * gain[:, span]
            mixed[rows, span] = out.astype(BF16)


def finish_pass(order, place, squares, gain, came):
    devices, height, lanes = came.shape
    blocks = order.shape[0] // devices
    width = gain.shape[1]
    each = FINISH_EACH

    def part(inside):
        def loader(b, order, place):
            return order[place[0] * blocks + b * each + inside] // blocks, 0, 0

        return pl.BlockSpec((1, width, lanes), loader)

    return pl.pallas_call(
        lambda *refs: finish_kernel(len(squares), each, *refs),
        grid_spec=pltpu.PrefetchScalarGridSpec(
            num_scalar_prefetch=2,
            grid=(blocks // each,),
            in_specs=[pl.BlockSpec((blocks, BLOCK), lambda b, *_: (0, 0))] * len(squares)
            + [pl.BlockSpec((1, width), lambda b, *_: (0, 0))]
            + [part(inside) for inside in range(each)],
            out_specs=pl.BlockSpec((each * BLOCK, width), lambda b, *_: (b, 0)),
        ),
        out_shape=jax.ShapeDtypeStruct((blocks * BLOCK, width), BF16),
        compiler_params=pltpu.CompilerParams(vmem_limit_bytes=14 * 2**20),
        name="finish",
    )(order, place, *squares, gain, *[came] * each)


def swap(x, axis):
    return lax.all_to_all(x, axis, split_axis=0, concat_axis=0, tiled=True)


def body(queries, key_rows, value_rows, log_decay, norm_gain, doc_lengths, packing):
    mine = lax.axis_index("ctx").astype(jnp.int32)
    place = mine.reshape(1)
    decay = log_decay.T
    lengths = doc_lengths[None, :]

    index = jnp.arange(packing.shape[0], dtype=jnp.int32)
    hit = (packing[None, :] == index[:, None]).astype(jnp.int32)
    order = jnp.sum(hit * index[None, :], axis=1)

    own = swap(own_states(packing, place, lengths, key_rows, value_rows, decay), "ctx")
    intra, faded = intra_pass(packing, place, lengths, queries, key_rows, value_rows, decay)

    own, order, intra, faded = lax.optimization_barrier((own, order, intra, faded))
    prior = scan_pass(order, own)
    prior, intra, faded = lax.optimization_barrier((prior, intra, faded))
    states = swap(prior, "ctx")
    came = swap(outgo_pass(packing, place, faded, intra, states), "ctx")
    part = squares_pass(order, place, came)
    groups = lax.axis_size("head")
    squares = [part]
    for shift in range(1, groups):
        pairs = [(i, (i + shift) % groups) for i in range(groups)]
        squares.append(lax.ppermute(part, "head", pairs))
    return finish_pass(order, place, squares, norm_gain[None, :], came)


def solution(mesh):
    placed = (
        P("ctx", "head"),
        P("ctx", "head"),
        P("ctx", "head"),
        P("ctx", "head"),
        P("head"),
        P(),
        P(),
    )
    return jax.shard_map(
        body, mesh=mesh, in_specs=placed, out_specs=P("ctx", "head"), check_vma=False
    )
```
